256 devices in a mesh: ctx: 32 (over y, z), head: 8 (over x, core).
Axes of the slice: x: 4, y: 4, z: 8, core: 2. Of those that a mesh axis runs over, the one named last changes fastest.
Arguments:
- queries: bfloat16 [16384, 4096], P('ctx', 'head'), may hold values from -6 to 6
- keys: bfloat16 [16384, 4096], P('ctx', 'head'), may hold values from -6 to 6
- values: bfloat16 [16384, 4096], P('ctx', 'head'), may hold values from -16 to 16
- out_grad: bfloat16 [16384, 4096], P('ctx', 'head'), may hold values from -6 to 6
- norm_gain: float32 [4096], P('head'), may hold values from 0.1 to 1.9
- doc_lengths: int32 [16], replicated, may hold values from 1 to 8192, 16384 in all
- group_level: int32 [8], replicated, may hold values from 0 to 2
Outputs:
- output: bfloat16 [16384, 4096], P('ctx', 'head')
- query_grad: bfloat16 [16384, 4096], P('ctx', 'head')
- key_grad: bfloat16 [16384, 4096], P('ctx', 'head')
- value_grad: bfloat16 [16384, 4096], P('ctx', 'head')
The draws below stay inside these ranges and needn't reach their ends.
All inputs are finite; a program needn't handle non-finite values.
Results may differ from the reference program's by a relative error of at most 0.013.
Values may be sent and summed in bfloat16 or wider, within the bound.
No kernel may reach another device: no remote copies, remote signals or barrier semaphores. Data moves between devices by JAX's collectives and lax.ppermute only.
A program may use at most 64 MiB of HBM per device.

```python
import math
import jax
import jax.numpy as jnp
import numpy as np
from jax import lax

HEAD_FEATURES = 128
HEAD_DEV = 4
SEGMENT = 512
DILATION = 32
DOCS = 16
SEQUENCE_TOKENS = 16384
HEADS = 32
WIDTH = 4096
GROUPS = 8
SELECTED = 512
DOC_MOST = 8192


def draw_queries(key, part):
    drawn = jnp.clip(jax.random.normal(jax.random.fold_in(key, 1), (SEQUENCE_TOKENS, WIDTH), jnp.float32), -6.0, 6.0)
    return drawn.astype(jnp.bfloat16)


def draw_keys(key, part):
    drawn = jnp.clip(jax.random.normal(jax.random.fold_in(key, 2), (SEQUENCE_TOKENS, WIDTH), jnp.float32), -6.0, 6.0)
    return drawn.astype(jnp.bfloat16)


def draw_values(key, part):
    head_of = jnp.arange(WIDTH) // HEAD_FEATURES
    ramp = head_of.astype(jnp.float32) / max(HEADS - 1, 1)
    drawn = jnp.clip(jax.random.normal(jax.random.fold_in(key, 5), (SEQUENCE_TOKENS, WIDTH), jnp.float32), -4.0, 4.0)
    return (drawn * (0.6 + 1.2 * ramp)).astype(jnp.bfloat16)


def with_ends(values, own_key, least, top_value):
    spot = [jax.random.randint(jax.random.fold_in(own_key, axis), (), 0, length) for axis, length in enumerate(values.shape)]
    main_axis = values.shape.index(max(values.shape))
    neighbour = spot[:main_axis] + [(spot[main_axis] + 1) % values.shape[main_axis]] + spot[main_axis + 1:]
    return values.at[tuple(spot)].set(least).at[tuple(neighbour)].set(top_value)


def shard_levels(rng, shape, pieces, low, high):
    loudness = 1.0
    for position, blocks in pieces:
        heights = jax.random.uniform(jax.random.fold_in(jax.random.fold_in(rng, 6), position), (blocks,), jnp.float32, low / len(pieces), high / len(pieces))
        loudness = loudness * jnp.repeat(jnp.exp(heights), shape[position] // blocks).reshape((-1,) + (1,) * (len(shape) - 1 - position))
    return loudness


def split_up(number_of, total, reach, slope):
    portions = [(1 << 20) // math.isqrt(rank ** slope) + 1 for rank in range(2, number_of + 1)]
    spare, counts = total - reach - (number_of - 1), [1] * (number_of - 1)
    while spare > 0:
        movable = [i for i in range(number_of - 1) if counts[i] < reach]
        mass, budget = sum([portions[i] for i in movable]), spare
        for i in movable:
            more = min(reach - counts[i], max(1, budget * portions[i] // mass), spare)
            counts[i] = counts[i] + more
            spare = spare - more
    return np.array([reach] + counts)


def uneven(own_key, number_of, total, reach, slope):
    if number_of == 2:
        one = jax.random.randint(own_key, (), max(1, total - reach), min(reach, total - 1) + 1)
        return jnp.stack([one, total - one])
    sizes = jnp.asarray(split_up(number_of, total, reach, slope), jnp.int32)
    couples = (number_of - 1) // 2
    giver, taker = sizes[1:1 + 2 * couples:2], sizes[2:2 + 2 * couples:2]
    slack = jnp.minimum(giver - 1, reach - taker)
    shifted = jax.random.randint(jax.random.fold_in(own_key, 1), (couples,), 0, 1 << 20) % (slack + 1)
    sizes = sizes.at[1:1 + 2 * couples:2].set(giver - shifted).at[2:2 + 2 * couples:2].set(taker + shifted)
    return sizes[jax.random.permutation(jax.random.fold_in(own_key, 2), number_of)]


def normal_values(key, dims, deviation, limit, cuts=(), kind=jnp.bfloat16):
    array = deviation * jax.random.normal(key, dims, jnp.float32)
    if cuts:
        array = array * shard_levels(key, dims, cuts, -0.22, 0.18)
    return jnp.clip(array, -limit, limit).astype(kind)


def setup_inputs(seed: int = 0) -> dict:
    arg_keys = jax.random.split(jax.random.key(seed), 8)
    return {
        "queries": draw_queries(jax.random.fold_in(arg_keys[7], 71), 0),
        "keys": draw_keys(jax.random.fold_in(arg_keys[7], 71), 0),
        "values": draw_values(jax.random.fold_in(arg_keys[7], 71), 0),
        "out_grad": normal_values(arg_keys[3], (SEQUENCE_TOKENS, WIDTH), 1.0, 6.0, ((0, 32), (1, 8))),
        "norm_gain": jnp.clip(1.0 + 0.18 * jax.random.normal(arg_keys[4], (WIDTH,), jnp.float32), 0.1, 1.9),
        "doc_lengths": uneven(arg_keys[5], DOCS, SEQUENCE_TOKENS, DOC_MOST, 2).astype(jnp.int32),
        "group_level": with_ends(jax.random.randint(arg_keys[6], (GROUPS,), 0, 3), jax.random.fold_in(arg_keys[6], 1), 0, 2).astype(jnp.int32),
    }


EPS = 1e-05

def document_of(places, doc_lengths):
    ends = jnp.cumsum(doc_lengths, dtype=jnp.int32)
    return lax.optimization_barrier(jnp.sum((places[..., None] >= ends).astype(jnp.int32), axis=-1, dtype=jnp.int32))

def head_masks(head, doc_lengths, group_level):
    offset = (head % DILATION).astype(jnp.int32)
    rate = jnp.left_shift(jnp.int32(1), group_level[head // HEAD_DEV].astype(jnp.int32))
    places = jnp.arange(SEQUENCE_TOKENS, dtype=jnp.int32)
    docs = document_of(places, doc_lengths)
    counter = jnp.arange(SELECTED, dtype=jnp.int32)
    far_places = counter * DILATION + offset
    far_docs = document_of(far_places, doc_lengths)
    local_places = places.reshape(SEQUENCE_TOKENS // SEGMENT, SEGMENT)
    local_docs = docs.reshape(SEQUENCE_TOKENS // SEGMENT, SEGMENT)
    near_mask = (local_places[:, :, None] >= local_places[:, None, :]) & (local_docs[:, :, None] == local_docs[:, None, :])
    far_mask = (far_places[None, :] <= places[:, None]) & (far_docs[None, :] == docs[:, None]) & (counter % rate == 0)[None, :]
    return (offset, near_mask, far_mask.reshape(SEQUENCE_TOKENS // SEGMENT, SEGMENT, SELECTED))

def pick_rows(rows, offset):
    return lax.dynamic_index_in_dim(rows.reshape(SELECTED, DILATION, HEAD_FEATURES), offset, axis=1, keepdims=False)

def weights_of(query_head, key_head, head, doc_lengths, group_level):
    offset, near_mask, far_mask = head_masks(head, doc_lengths, group_level)
    logit_scale = HEAD_FEATURES ** (-0.5)
    query_tiles = query_head.reshape(SEQUENCE_TOKENS // SEGMENT, SEGMENT, HEAD_FEATURES)
    key_tiles = key_head.reshape(SEQUENCE_TOKENS // SEGMENT, SEGMENT, HEAD_FEATURES)
    far_keys = pick_rows(key_head, offset)
    nearby_logit = jnp.einsum('vlr,vwr->vlw', query_tiles.astype(jnp.float32), key_tiles.astype(jnp.float32)) * logit_scale
    far_score = jnp.dot(query_head, far_keys.T, preferred_element_type=jnp.float32).reshape(SEQUENCE_TOKENS // SEGMENT, SEGMENT, SELECTED) * logit_scale
    top = jnp.maximum(lax.optimization_barrier(jnp.max(jnp.where(near_mask, nearby_logit, -jnp.inf), -1)), lax.optimization_barrier(jnp.max(jnp.where(far_mask, far_score, -jnp.inf), -1)))
    summed = lax.optimization_barrier(jnp.sum(jnp.where(near_mask, jnp.exp(nearby_logit - top[..., None]), 0.0), -1)) + lax.optimization_barrier(jnp.sum(jnp.where(far_mask, jnp.exp(far_score - top[..., None]), 0.0), -1))
    log_total = top + jnp.log(summed)
    nearby_weight = jnp.where(near_mask, jnp.exp(nearby_logit - log_total[..., None]), 0.0)
    far_weight = jnp.where(far_mask, jnp.exp(far_score - log_total[..., None]), 0.0)
    return (nearby_weight, far_weight, offset)

def reference(queries, keys, values, out_grad, norm_gain, doc_lengths, group_level):
    logit_scale = HEAD_FEATURES ** (-0.5)

    def split(rows):
        return rows.reshape(SEQUENCE_TOKENS, HEADS, HEAD_FEATURES).transpose(1, 0, 2)

    def merge(rows):
        return rows.transpose(1, 0, 2).reshape(SEQUENCE_TOKENS, WIDTH)

    def forward_head(inputs):
        query_head, key_head, value_head, head = inputs
        nearby_weight, far_weight, offset = weights_of(query_head, key_head, head, doc_lengths, group_level)
        value_tiles = value_head.reshape(SEQUENCE_TOKENS // SEGMENT, SEGMENT, HEAD_FEATURES)
        far_values = pick_rows(value_head, offset)
        nearby_portion = jnp.einsum('xen,xna->xea', nearby_weight.astype(jnp.bfloat16).astype(jnp.float32), value_tiles.astype(jnp.float32)).reshape(SEQUENCE_TOKENS, HEAD_FEATURES)
        far_part = jnp.dot(far_weight.reshape(SEQUENCE_TOKENS, SELECTED).astype(jnp.bfloat16), far_values, preferred_element_type=jnp.float32)
        return (nearby_portion + far_part).astype(jnp.bfloat16)
    head_ids = jnp.arange(HEADS, dtype=jnp.int32)
    attended = merge(lax.map(forward_head, (split(queries), split(keys), split(values), head_ids)))
    flat = attended.astype(jnp.float32)
    mean = lax.optimization_barrier(jnp.sum(flat, 1)) / WIDTH
    rstd = lax.rsqrt(lax.optimization_barrier(jnp.sum(flat * flat, 1)) / WIDTH - mean * mean + EPS)
    normed = (flat - mean[:, None]) * rstd[:, None]
    output = (normed * norm_gain).astype(jnp.bfloat16)
    scaled = out_grad.astype(jnp.float32) * norm_gain
    grad_mean = lax.optimization_barrier(jnp.sum(scaled, 1)) / WIDTH
    grad_proj = lax.optimization_barrier(jnp.sum(scaled * normed, 1)) / WIDTH
    att_grad = (rstd[:, None] * (scaled - grad_mean[:, None] - normed * grad_proj[:, None])).astype(jnp.bfloat16)

    def backward_head(inputs):
        query_head, key_head, value_head, attended_head, grad_head, head = inputs
        nearby_weight, far_weight, offset = weights_of(query_head, key_head, head, doc_lengths, group_level)
        blocks = SEQUENCE_TOKENS // SEGMENT
        query_tiles = query_head.reshape(blocks, SEGMENT, HEAD_FEATURES).astype(jnp.float32)
        key_tiles = key_head.reshape(blocks, SEGMENT, HEAD_FEATURES).astype(jnp.float32)
        value_tiles = value_head.reshape(blocks, SEGMENT, HEAD_FEATURES).astype(jnp.float32)
        gradient_tiles = grad_head.reshape(blocks, SEGMENT, HEAD_FEATURES).astype(jnp.float32)
        far_keys = pick_rows(key_head, offset)
        far_values = pick_rows(value_head, offset)
        delta = lax.optimization_barrier(jnp.sum(attended_head.astype(jnp.float32) * grad_head.astype(jnp.float32), -1)).reshape(blocks, SEGMENT)
        nearby_product = jnp.einsum('vlr,vwr->vlw', gradient_tiles, value_tiles)
        far_dot = jnp.dot(grad_head, far_values.T, preferred_element_type=jnp.float32).reshape(blocks, SEGMENT, SELECTED)
        nearby_gradient_slope = (nearby_weight * (nearby_product - delta[..., None])).astype(jnp.bfloat16)
        far_slope = (far_weight * (far_dot - delta[..., None])).astype(jnp.bfloat16).reshape(SEQUENCE_TOKENS, SELECTED)
        nearby_rounded = nearby_weight.astype(jnp.bfloat16).astype(jnp.float32)
        far_round = far_weight.astype(jnp.bfloat16).reshape(SEQUENCE_TOKENS, SELECTED)
        query_portion = jnp.einsum('xen,xna->xea', nearby_gradient_slope.astype(jnp.float32), key_tiles).reshape(SEQUENCE_TOKENS, HEAD_FEATURES)
        query_portion = query_portion + jnp.dot(far_slope, far_keys, preferred_element_type=jnp.float32)
        nearby_key = jnp.einsum('nsa,nsx->nax', nearby_gradient_slope.astype(jnp.float32), query_tiles).reshape(SEQUENCE_TOKENS, HEAD_FEATURES)
        nearby_value = jnp.einsum('nsa,nsx->nax', nearby_rounded, gradient_tiles).reshape(SEQUENCE_TOKENS, HEAD_FEATURES)
        far_key = jnp.dot(far_slope.T, query_head, preferred_element_type=jnp.float32)
        far_value = jnp.dot(far_round.T, grad_head, preferred_element_type=jnp.float32)
        place = (jnp.arange(DILATION, dtype=jnp.int32) == offset).astype(jnp.float32)

        def spread(near_rows, far_rows):
            return near_rows + (far_rows[:, None, :] * place[None, :, None]).reshape(SEQUENCE_TOKENS, HEAD_FEATURES)
        return ((query_portion * logit_scale).astype(jnp.bfloat16), (spread(nearby_key, far_key) * logit_scale).astype(jnp.bfloat16), spread(nearby_value, far_value).astype(jnp.bfloat16))
    query_grad, key_grad, value_grad = lax.map(backward_head, (split(queries), split(keys), split(values), split(attended), split(att_grad), head_ids))
    return (output, merge(query_grad), merge(key_grad), merge(value_grad))
```

```python
import jax
import jax.numpy as jnp
from jax import lax
from jax.experimental import pallas as pl
from jax.experimental.pallas import tpu as pltpu
from jax.sharding import PartitionSpec as P

D = 128
HEADS = 4
TOK = 512
WIDE = HEADS * D
DILATION = 32
DOCS = 16
PICK = TOK // DILATION
ZN = 8
YN = 4
FAR = 17 * PICK
HALF = 256
FULL = 4096.0
EPS = 1e-05
SCALE = D ** (-0.5)
C2 = SCALE * 1.4426950408889634
NEG = -1e30


F32 = jnp.float32
BF16 = jnp.bfloat16


def nn(a, b):
    return lax.dot_general(a, b, (((1,), (0,)), ((), ())), preferred_element_type=F32)


def nt(a, b):
    return lax.dot_general(a, b, (((1,), (1,)), ((), ())), preferred_element_type=F32)


def tn(a, b):
    return lax.dot_general(a, b, (((0,), (0,)), ((), ())), preferred_element_type=F32)


def cols(h):
    return slice(h * D, (h + 1) * D)


def query_rows(ids, lens):
    place = ids[0] * TOK + lax.broadcasted_iota(jnp.int32, (1, TOK), 1)
    start = jnp.zeros((1, TOK), jnp.int32)
    end = jnp.int32(0)
    for k in range(DOCS):
        end = end + lens[k]
        start = jnp.where(place >= end, end, start)
    return place, start


def near_bias(place, start, at, depth):
    base = place[:, 0:1]
    key = lax.broadcasted_iota(jnp.int32, (depth, HALF), 0)
    query = place[:, at : at + HALF] - base
    first = start[:, at : at + HALF] - base
    return jnp.where((key <= query) & (key >= first), 0.0, NEG)


def far_places(ids, levels):
    row = lax.broadcasted_iota(jnp.int32, (FAR, 1), 0)
    block = lax.shift_right_logical(row, 4)
    t = row & 15
    z = ids[0] & 7
    y = lax.shift_right_logical(ids[0], 3)
    from_z = lax.shift_right_logical(block, 1)
    slot = block & 1
    at = (y - slot - jnp.where(from_z > z, 1, 0)) * ZN + from_z
    at = jnp.where(block == 16, (y - 2) * ZN + z, at)
    rate = lax.shift_left(jnp.int32(1), levels[ids[1]])
    return jnp.where((t & (rate - 1)) == 0, at * TOK + t * DILATION, -(1 << 29))


def far_live(fplace, place, start, offset, at):
    q = place[:, at : at + HALF] - offset
    s = start[:, at : at + HALF] - offset
    return (fplace <= q) & (fplace >= s)


def pick_kernel(ids, k, v, out):
    row = lax.broadcasted_iota(jnp.int32, (PICK, TOK), 0) * DILATION
    col = lax.broadcasted_iota(jnp.int32, (PICK, TOK), 1)
    for h in range(HEADS):
        one = jnp.where(col == row + (ids[1] * HEADS + h), 1.0, 0.0).astype(BF16)
        out[0, :, cols(h)] = nn(one, k[:, cols(h)]).astype(BF16)
        out[1, :, cols(h)] = nn(one, v[:, cols(h)]).astype(BF16)


def bundle_kernel(ids, own, r1, r2, out):
    z = ids[0] & 7
    for d in range(ZN):
        up = d >= z
        for kv in range(2):
            out[d, kv, 0:PICK] = jnp.where(up, own[kv], r1[kv])
            out[d, kv, PICK : 2 * PICK] = jnp.where(up, r1[kv], r2[kv])


def near_forward_kernel(ids, lens, q, k, v, g, gain, acc, rows, scaled):
    place, start = query_rows(ids, lens)
    for at in range(0, TOK, HALF):
        depth = at + HALF
        bias = near_bias(place, start, at, depth)
        for h in range(HEADS):
            s = nt(k[:depth, cols(h)], q[at : at + HALF, cols(h)]) * C2 + bias
            top = jnp.max(s, axis=0, keepdims=True)
            p = jnp.exp2(s - top)
            rows[h : h + 1, at : at + HALF] = top
            rows[HEADS + h : HEADS + h + 1, at : at + HALF] = jnp.sum(p, axis=0, keepdims=True)
            acc[cols(h), at : at + HALF] = tn(v[:depth, cols(h)], p.astype(BF16))
    total = jnp.zeros((1, TOK), F32)
    for h in range(HEADS):
        part = (g[:, cols(h)].astype(F32) * gain[:, cols(h)]).T
        scaled[cols(h), :] = part
        total = total + jnp.sum(part, axis=0, keepdims=True)
    rows[8:9, :] = total
    rows[9:16, :] = jnp.zeros((7, TOK), F32)


def far_of(x, r2, kv, h):
    return jnp.concatenate(
        [x[:, kv, :, cols(h)].reshape(ZN * 2 * PICK, D), r2[kv, :, cols(h)]], axis=0
    )


def far_forward_kernel(ids, lens, levels, x, r2, q, acc, rows, scaled, flat, stats, totals):
    place, start = query_rows(ids, lens)
    fplace = far_places(ids, levels)
    for at in range(0, TOK, HALF):
        part = slice(at, at + HALF)
        sums = jnp.zeros((1, HALF), F32)
        squares = jnp.zeros((1, HALF), F32)
        cross = jnp.zeros((1, HALF), F32)
        for h in range(HEADS):
            live = far_live(fplace, place, start, ids[1] * HEADS + h, at)
            s = jnp.where(live, nt(far_of(x, r2, 0, h), q[part, cols(h)]) * C2, NEG)
            near_top = rows[h : h + 1, part]
            top = jnp.maximum(near_top, jnp.max(s, axis=0, keepdims=True))
            p = jnp.exp2(s - top)
            shrink = jnp.exp2(near_top - top)
            total = rows[HEADS + h : HEADS + h + 1, part] * shrink + jnp.sum(
                p, axis=0, keepdims=True
            )
            o = acc[cols(h), part] * shrink + tn(far_of(x, r2, 1, h), p.astype(BF16))
            o = (o * (1.0 / total)).astype(BF16)
            flat[cols(h), part] = o
            totals[h : h + 1, part] = top + jnp.log2(total)
            f = o.astype(F32)
            sums = sums + jnp.sum(f, axis=0, keepdims=True)
            squares = squares + jnp.sum(f * f, axis=0, keepdims=True)
            cross = cross + jnp.sum(f * scaled[cols(h), part], axis=0, keepdims=True)
        stats[0:1, part] = sums
        stats[1:2, part] = squares
        stats[2:3, part] = rows[8:9, part]
        stats[3:4, part] = cross
    stats[4:8, :] = jnp.zeros((4, TOK), F32)
    totals[4:8, :] = jnp.zeros((4, TOK), F32)


def norm_rows(s0, s1, s2, s3, part):
    tot = (s0[:, part] + s1[:, part]) + (s2[:, part] + s3[:, part])
    mean = tot[0:1] / FULL
    rstd = lax.rsqrt(tot[1:2] / FULL - mean * mean + EPS)
    grad_mean = tot[2:3] / FULL
    grad_proj = rstd * (tot[3:4] - mean * tot[2:3]) / FULL
    return mean, rstd, grad_mean, grad_proj


def att_grad_of(flat, scaled, norm, h, part):
    mean, rstd, grad_mean, grad_proj = norm
    f = flat[cols(h), part].astype(F32)
    normed = (f - mean) * rstd
    grad = (rstd * (scaled[cols(h), part] - grad_mean - normed * grad_proj)).astype(BF16)
    delta = jnp.sum(grad.astype(F32) * f, axis=0, keepdims=True)
    return grad, delta, normed


def far_backward_kernel(
    ids, lens, levels, s0, s1, s2, s3, x, r2, q, flat, scaled, totals, out, own, kacc, vacc
):
    place, start = query_rows(ids, lens)
    fplace = far_places(ids, levels)
    for h in range(HEADS):
        fk, fv = far_of(x, r2, 0, h), far_of(x, r2, 1, h)
        key_part = jnp.zeros((FAR, D), F32)
        value_part = jnp.zeros((FAR, D), F32)
        for at in range(0, TOK, HALF):
            part = slice(at, at + HALF)
            norm = norm_rows(s0, s1, s2, s3, part)
            grad, delta, _ = att_grad_of(flat, scaled, norm, h, part)
            live = far_live(fplace, place, start, ids[1] * HEADS + h, at)
            s = jnp.where(live, nt(fk, q[part, cols(h)]) * C2, NEG)
            p = jnp.exp2(s - totals[h : h + 1, part])
            slope = (p * (nn(fv, grad) - delta)).astype(BF16)
            key_part = key_part + nn(slope, q[part, cols(h)])
            value_part = value_part + nt(p.astype(BF16), grad)
        kacc[...] = key_part * SCALE
        vacc[...] = value_part
        for d in range(ZN):
            at = d * 2 * PICK
            out[d, 0, :, cols(h)] = kacc[at : at + 2 * PICK, :].astype(BF16)
            out[d, 1, :, cols(h)] = vacc[at : at + 2 * PICK, :].astype(BF16)
        own[0, :, cols(h)] = kacc[FAR - PICK : FAR, :]
        own[1, :, cols(h)] = vacc[FAR - PICK : FAR, :]


def near_backward_kernel(
    ids, lens, levels, s0, s1, s2, s3, x, r2, q, k, v, flat, scaled, totals, gain,
    output, query_grad, key_near, value_near,
):
    place, start = query_rows(ids, lens)
    fplace = far_places(ids, levels)
    for at in range(0, TOK, HALF):
        part = slice(at, at + HALF)
        depth = at + HALF
        bias = near_bias(place, start, at, depth)
        norm = norm_rows(s0, s1, s2, s3, part)
        for h in range(HEADS):
            grad, delta, normed = att_grad_of(flat, scaled, norm, h, part)
            output[part, cols(h)] = (normed.T * gain[:, cols(h)]).astype(BF16)
            qh = q[part, cols(h)]
            top = totals[h : h + 1, part]
            kh, vh = k[:depth, cols(h)], v[:depth, cols(h)]
            p = jnp.exp2(nt(kh, qh) * C2 + bias - top)
            slope = (p * (nn(vh, grad) - delta)).astype(BF16)
            key_part = nn(slope, qh) * SCALE
            value_part = nt(p.astype(BF16), grad)
            if at == 0:
                key_near[:depth, cols(h)] = key_part
                value_near[:depth, cols(h)] = value_part
            else:
                key_near[:at, cols(h)] += key_part[:at]
                value_near[:at, cols(h)] += value_part[:at]
                key_near[at:, cols(h)] = key_part[at:]
                value_near[at:, cols(h)] = value_part[at:]
            query_part = tn(kh, slope)
            fk, fv = far_of(x, r2, 0, h), far_of(x, r2, 1, h)
            live = far_live(fplace, place, start, ids[1] * HEADS + h, at)
            s = jnp.where(live, nt(fk, qh) * C2, NEG)
            p = jnp.exp2(s - top)
            slope = (p * (nn(fv, grad) - delta)).astype(BF16)
            query_part = query_part + tn(fk, slope)
            query_grad[part, cols(h)] = (query_part.T * SCALE).astype(BF16)


def gather_kernel(ids, x, r2_part, own, back1, back2):
    z = ids[0] & 7
    for kv in range(2):
        a = jnp.zeros((PICK, WIDE), F32)
        b = jnp.zeros((PICK, WIDE), F32)
        c = r2_part[kv]
        for d in range(ZN):
            up = d >= z
            low = x[d, kv, 0:PICK].astype(F32)
            high = x[d, kv, PICK : 2 * PICK].astype(F32)
            a = a + jnp.where(up, low, 0.0)
            b = b + jnp.where(up, high, low)
            c = c + jnp.where(up, 0.0, high)
        own[kv] = a
        back1[kv] = b.astype(BF16)
        back2[kv] = c.astype(BF16)


def finish_kernel(ids, own, back1, back2, key_near, value_near, key_grad, value_grad):
    inner = lax.broadcasted_iota(jnp.int32, (PICK, DILATION, D), 1)
    for kv, near, out in ((0, key_near, key_grad), (1, value_near, value_grad)):
        for h in range(HEADS):
            far = (
                own[kv, :, cols(h)]
                + back1[kv, :, cols(h)].astype(F32)
                + back2[kv, :, cols(h)].astype(F32)
            )
            wide = jnp.where(inner == ids[1] * HEADS + h, far[:, None, :], 0.0)
            out[:, cols(h)] = (near[:, cols(h)] + wide.reshape(TOK, D)).astype(BF16)


SMEM = pl.BlockSpec(memory_space=pltpu.SMEM)
VMEM = pl.BlockSpec(memory_space=pltpu.VMEM)


def call(kernel, n_small, args, outs, scratch=(), flops=0, nbytes=0):
    return pl.pallas_call(
        kernel,
        out_shape=tuple(jax.ShapeDtypeStruct(s, t) for s, t in outs),
        in_specs=[SMEM] * n_small + [VMEM] * (len(args) - n_small),
        out_specs=tuple(VMEM for _ in outs),
        scratch_shapes=scratch,
        compiler_params=pltpu.CompilerParams(vmem_limit_bytes=32 << 20),
        cost_estimate=pl.CostEstimate(flops=flops, bytes_accessed=nbytes, transcendentals=0),
    )(*args)


def along_y(step):
    return [(y * ZN + z, (y + step) % YN * ZN + z) for y in range(YN) for z in range(ZN)]


Z_GROUPS = [[y * ZN + z for z in range(ZN)] for y in range(YN)]


def along_x(step):
    return [(p, (p + 2 * step) % 8) for p in range(8)]


def shards(queries, keys, values, out_grad, norm_gain, doc_lengths, group_level):
    two = jnp.arange(2, dtype=jnp.int32)
    ids = jnp.where(two == 0, lax.axis_index("ctx"), lax.axis_index("head")).astype(jnp.int32)
    gain = norm_gain.reshape(1, WIDE)
    bundle = (2, PICK, WIDE)
    block = (ZN, 2, 2 * PICK, WIDE)
    square = (TOK, WIDE)

    (mine,) = call(pick_kernel, 1, (ids, keys, values), [(bundle, BF16)], nbytes=1 << 20)
    r1 = lax.ppermute(mine, "ctx", along_y(1))
    r2 = lax.ppermute(mine, "ctx", along_y(2))
    (sent,) = call(bundle_kernel, 1, (ids, mine, r1, r2), [(block, BF16)], nbytes=1 << 19)
    x = lax.all_to_all(sent, "ctx", 0, 0, axis_index_groups=Z_GROUPS, tiled=True)

    acc, rows, scaled = call(
        near_forward_kernel,
        2,
        (ids, doc_lengths, queries, keys, values, out_grad, gain),
        [((WIDE, TOK), F32), ((16, TOK), F32), ((WIDE, TOK), F32)],
        flops=4 * 4 * TOK * TOK * D,
        nbytes=4 << 20,
    )
    flat, stats, totals = call(
        far_forward_kernel,
        3,
        (ids, doc_lengths, group_level, x, r2, queries, acc, rows, scaled),
        [((WIDE, TOK), BF16), ((8, TOK), F32), ((8, TOK), F32)],
        flops=4 * 4 * TOK * FAR * D,
        nbytes=4 << 20,
    )
    s0 = stats + lax.ppermute(stats, "head", [(p, p ^ 1) for p in range(8)])
    s1, s2, s3 = (lax.ppermute(s0, "head", along_x(k)) for k in (1, 2, 3))
    back, back_own = call(
        far_backward_kernel,
        3,
        (ids, doc_lengths, group_level, s0, s1, s2, s3, x, r2, queries, flat, scaled, totals),
        [(block, BF16), (bundle, F32)],
        scratch=[pltpu.VMEM((FAR, D), F32), pltpu.VMEM((FAR, D), F32)],
        flops=8 * 4 * TOK * FAR * D,
        nbytes=4 << 20,
    )
    arrived = lax.all_to_all(back, "ctx", 0, 0, axis_index_groups=Z_GROUPS, tiled=True)
    output, query_grad, key_near, value_near = call(
        near_backward_kernel,
        3,
        (
            ids, doc_lengths, group_level, s0, s1, s2, s3, x, r2,
            queries, keys, values, flat, scaled, totals, gain,
        ),
        [(square, BF16), (square, BF16), (square, F32), (square, F32)],
        flops=16 * 4 * TOK * TOK * D,
        nbytes=8 << 20,
    )
    own, back1, back2 = call(
        gather_kernel,
        1,
        (ids, arrived, back_own),
        [(bundle, F32), (bundle, BF16), (bundle, BF16)],
        nbytes=1 << 20,
    )
    back1 = lax.ppermute(back1, "ctx", along_y(-1))
    back2 = lax.ppermute(back2, "ctx", along_y(-2))
    key_grad, value_grad = call(
        finish_kernel,
        1,
        (ids, own, back1, back2, key_near, value_near),
        [(square, BF16), (square, BF16)],
        nbytes=3 << 20,
    )
    return output, query_grad, key_grad, value_grad


def solution(mesh):
    tokens = P("ctx", "head")
    return jax.shard_map(
        shards,
        mesh=mesh,
        in_specs=(tokens, tokens, tokens, tokens, P("head"), P(), P()),
        out_specs=(tokens, tokens, tokens, tokens),
        check_vma=False,
    )
```

```python
import jax
import jax.numpy as jnp
from jax import lax
from jax.experimental import pallas as pl
from jax.experimental.pallas import tpu as pltpu
from jax.sharding import PartitionSpec as P

D = 128
HEADS = 4
TOK = 512
WIDE = HEADS * D
DILATION = 32
DOCS = 16
PICK = TOK // DILATION
ZN = 8
YN = 4
FAR = 17 * PICK
HALF = 256
FULL = 4096.0
EPS = 1e-05
SCALE = D ** (-0.5)
C2 = SCALE * 1.4426950408889634
NEG = -1e30
LIMIT = 8 << 20
NEAR_FIRST = True
BACK_FIRST = False
OUT_ORDER = (0, 1, 2, 3, 4, 5, 6, 7)
BACK_ORDER = (7, 6, 5, 4, 3, 2, 1, 0)


F32 = jnp.float32
BF16 = jnp.bfloat16


def nn(a, b):
    return lax.dot_general(a, b, (((1,), (0,)), ((), ())), preferred_element_type=F32)


def nt(a, b):
    return lax.dot_general(a, b, (((1,), (1,)), ((), ())), preferred_element_type=F32)


def tn(a, b):
    return lax.dot_general(a, b, (((0,), (0,)), ((), ())), preferred_element_type=F32)


def cols(h):
    return slice(h * D, (h + 1) * D)


def query_rows(ids, lens):
    place = ids[0] * TOK + lax.broadcasted_iota(jnp.int32, (1, TOK), 1)
    start = jnp.zeros((1, TOK), jnp.int32)
    end = jnp.int32(0)
    for k in range(DOCS):
        end = end + lens[k]
        start = jnp.where(place >= end, end, start)
    return place, start


def near_bias(place, start, at, depth):
    base = place[:, 0:1]
    key = lax.broadcasted_iota(jnp.int32, (depth, HALF), 0)
    query = place[:, at : at + HALF] - base
    first = start[:, at : at + HALF] - base
    return jnp.where((key <= query) & (key >= first), 0.0, NEG)


def far_places(ids, levels):
    row = lax.broadcasted_iota(jnp.int32, (FAR, 1), 0)
    block = lax.shift_right_logical(row, 4)
    t = row & 15
    z = ids[0] & 7
    y = lax.shift_right_logical(ids[0], 3)
    slot_of = lax.shift_right_logical(block, 1)
    from_z = jnp.zeros_like(slot_of)
    for d, z_of in enumerate(OUT_ORDER):
        from_z = jnp.where(slot_of == d, z_of, from_z)
    slot = block & 1
    at = (y - slot - jnp.where(from_z > z, 1, 0)) * ZN + from_z
    at = jnp.where(block == 16, (y - 2) * ZN + z, at)
    rate = lax.shift_left(jnp.int32(1), levels[ids[1]])
    return jnp.where((t & (rate - 1)) == 0, at * TOK + t * DILATION, -(1 << 29))


def pick_kernel(ids, k, v, out, kbuf, vbuf, sems):
    group = lax.shift_right_logical(ids[1] * HEADS, 3)
    copies = [
        pltpu.make_async_copy(k.at[:, group], kbuf, sems.at[0]),
        pltpu.make_async_copy(v.at[:, group], vbuf, sems.at[1]),
    ]
    for copy in copies:
        copy.start()
    row = lax.broadcasted_iota(jnp.int32, (PICK, PICK * 8), 0) * 8
    col = lax.broadcasted_iota(jnp.int32, (PICK, PICK * 8), 1)
    first = (ids[1] * HEADS) & 7
    for kv, buf in enumerate((kbuf, vbuf)):
        copies[kv].wait()
        for h in range(HEADS):
            one = jnp.where(col == row + (first + h), 1.0, 0.0).astype(BF16)
            rows = buf[:, :, cols(h)].astype(F32).reshape(PICK * 8, D).astype(BF16)
            out[kv, :, cols(h)] = nn(one, rows).astype(BF16)


def bundle_kernel(ids, own, r1, r2, out):
    z = ids[0] & 7
    for d in range(ZN):
        up = OUT_ORDER[d] >= z
        for kv in range(2):
            out[d, kv, 0:PICK] = jnp.where(up, own[kv], r1[kv])
            out[d, kv, PICK : 2 * PICK] = jnp.where(up, r1[kv], r2[kv])


def near_forward_kernel(
    ids, lens_at, levels_at, q_at, k_at, v_at, g_at, gain_at,
    acc, rows, scaled, fbias, nbias, q, k, v, gain, g, lens, levels, sems,
):
    pairs = (
        (lens_at, lens), (levels_at, levels), (q_at, q), (k_at, k), (v_at, v), (g_at, g),
        (gain_at, gain),
    )
    copies = [pltpu.make_async_copy(a, b, sems.at[i]) for i, (a, b) in enumerate(pairs)]
    for copy in copies:
        copy.start()
    for copy in copies[:2]:
        copy.wait()
    place, start = query_rows(ids, lens)
    fplace = far_places(ids, levels)
    for h in range(HEADS):
        offset = ids[1] * HEADS + h
        live = (fplace <= place - offset) & (fplace >= start - offset)
        fbias[h] = jnp.where(live, 0.0, NEG)
    for at in range(0, TOK, HALF):
        nbias[: at + HALF, at : at + HALF] = near_bias(place, start, at, at + HALF)
    nbias[HALF:, :HALF] = jnp.full((HALF, HALF), NEG, F32)
    for copy in copies[2:]:
        copy.wait()
    for h in range(HEADS):
        for at in range(0, TOK, HALF):
            depth = at + HALF
            s = nt(k[:depth, cols(h)], q[at:depth, cols(h)]) * C2 + nbias[:depth, at:depth]
            top = jnp.max(s, axis=0, keepdims=True)
            p = jnp.exp2(s - top)
            rows[h : h + 1, at:depth] = top
            rows[HEADS + h : HEADS + h + 1, at:depth] = jnp.sum(p, axis=0, keepdims=True)
            acc[cols(h), at:depth] = tn(v[:depth, cols(h)], p.astype(BF16))
    total = jnp.zeros((1, TOK), F32)
    for h in range(HEADS):
        part = (g[:, cols(h)].astype(F32) * gain[:, cols(h)]).T
        scaled[cols(h), :] = part
        total = total + jnp.sum(part, axis=0, keepdims=True)
    rows[8:9, :] = total
    rows[9:16, :] = jnp.zeros((7, TOK), F32)


def far_of(x, r2, kv, h):
    return jnp.concatenate(
        [x[:, kv, :, cols(h)].reshape(ZN * 2 * PICK, D), r2[kv, :, cols(h)]], axis=0
    )


def far_forward_kernel(x, r2, q, acc, rows, scaled, fbias, flat, stats, totals):
    for at in range(0, TOK, HALF):
        part = slice(at, at + HALF)
        sums = jnp.zeros((1, HALF), F32)
        squares = jnp.zeros((1, HALF), F32)
        cross = jnp.zeros((1, HALF), F32)
        for h in range(HEADS):
            s = nt(far_of(x, r2, 0, h), q[part, cols(h)]) * C2 + fbias[h, :, part]
            near_top = rows[h : h + 1, part]
            top = jnp.maximum(near_top, jnp.max(s, axis=0, keepdims=True))
            p = jnp.exp2(s - top)
            shrink = jnp.exp2(near_top - top)
            total = rows[HEADS + h : HEADS + h + 1, part] * shrink + jnp.sum(
                p, axis=0, keepdims=True
            )
            o = acc[cols(h), part] * shrink + tn(far_of(x, r2, 1, h), p.astype(BF16))
            o = (o * (1.0 / total)).astype(BF16)
            flat[cols(h), part] = o
            totals[h : h + 1, part] = top + jnp.log2(total)
            f = o.astype(F32)
            sums = sums + jnp.sum(f, axis=0, keepdims=True)
            squares = squares + jnp.sum(f * f, axis=0, keepdims=True)
            cross = cross + jnp.sum(f * scaled[cols(h), part], axis=0, keepdims=True)
        stats[0:1, part] = sums
        stats[1:2, part] = squares
        stats[2:3, part] = rows[8:9, part]
        stats[3:4, part] = cross
    stats[4:8, :] = jnp.zeros((4, TOK), F32)
    totals[4:8, :] = jnp.zeros((4, TOK), F32)


def weight_kernel(x, r2, q, k, totals, fbias, nbias, far_weight, near_weight):
    for h in range(HEADS):
        fk = far_of(x, r2, 0, h)
        for at in range(0, TOK, HALF):
            depth = at + HALF
            total = totals[h : h + 1, at:depth]
            qh = q[at:depth, cols(h)]
            far_weight[h, :, at:depth] = jnp.exp2(nt(fk, qh) * C2 + fbias[h, :, at:depth] - total)
            near_weight[h, :depth, at:depth] = jnp.exp2(
                nt(k[:depth, cols(h)], qh) * C2 + nbias[:depth, at:depth] - total
            )


def norm_rows(s0, s1, s2, s3, part):
    tot = (s0[:, part] + s1[:, part]) + (s2[:, part] + s3[:, part])
    mean = tot[0:1] / FULL
    rstd = lax.rsqrt(tot[1:2] / FULL - mean * mean + EPS)
    grad_mean = tot[2:3] / FULL
    grad_proj = rstd * (tot[3:4] - mean * tot[2:3]) / FULL
    return mean, rstd, grad_mean, grad_proj


def att_grad_of(flat, scaled, norm, h, part):
    mean, rstd, grad_mean, grad_proj = norm
    f = flat[cols(h), part].astype(F32)
    normed = (f - mean) * rstd
    grad = (rstd * (scaled[cols(h), part] - grad_mean - normed * grad_proj)).astype(BF16)
    delta = jnp.sum(grad.astype(F32) * f, axis=0, keepdims=True)
    return grad, delta, normed


def far_backward_kernel(s0, s1, s2, s3, x, r2, q, flat, scaled, weight, out, own, kacc, vacc):
    for h in range(HEADS):
        fv = far_of(x, r2, 1, h)
        key_part = jnp.zeros((FAR, D), F32)
        value_part = jnp.zeros((FAR, D), F32)
        for at in range(0, TOK, HALF):
            part = slice(at, at + HALF)
            norm = norm_rows(s0, s1, s2, s3, part)
            grad, delta, _ = att_grad_of(flat, scaled, norm, h, part)
            p = weight[h, :, part]
            slope = (p * (nn(fv, grad) - delta)).astype(BF16)
            key_part = key_part + nn(slope, q[part, cols(h)])
            value_part = value_part + nt(p.astype(BF16), grad)
        kacc[...] = key_part * SCALE
        vacc[...] = value_part
        for d in range(ZN):
            at = d * 2 * PICK
            to = BACK_ORDER.index(OUT_ORDER[d])
            out[to, 0, :, cols(h)] = kacc[at : at + 2 * PICK, :].astype(BF16)
            out[to, 1, :, cols(h)] = vacc[at : at + 2 * PICK, :].astype(BF16)
        own[0, :, cols(h)] = kacc[FAR - PICK : FAR, :]
        own[1, :, cols(h)] = vacc[FAR - PICK : FAR, :]


def near_backward_kernel(
    ids, s0, s1, s2, s3, x, r2, q, k, v, flat, scaled, far_weight, near_weight, gain,
    output, query_grad, key_grad, value_grad, tiles, kacc, vacc, bufs, sems,
):
    group = lax.shift_right_logical(ids[1] * HEADS, 3)
    norms = [norm_rows(s0, s1, s2, s3, slice(at, at + HALF)) for at in range(0, TOK, HALF)]
    copies = []
    for h in range(HEADS):
        for at in range(0, TOK, HALF):
            part = slice(at, at + HALF)
            depth = at + HALF
            grad, delta, normed = att_grad_of(flat, scaled, norms[at // HALF], h, part)
            bufs[0, part, cols(h)] = (normed.T * gain[:, cols(h)]).astype(BF16)
            qh = q[part, cols(h)]
            kh, vh = k[:depth, cols(h)], v[:depth, cols(h)]
            p = near_weight[h, :depth, part]
            slope = (p * (nn(vh, grad) - delta)).astype(BF16)
            key_part = nn(slope, qh)
            value_part = nt(p.astype(BF16), grad)
            if at == 0:
                kacc[:depth, :] = key_part
                vacc[:depth, :] = value_part
            else:
                kacc[:at, :] += key_part[:at]
                vacc[:at, :] += value_part[:at]
                kacc[at:, :] = key_part[at:]
                vacc[at:, :] = value_part[at:]
            query_part = tn(kh, slope)
            slope = (far_weight[h, :, part] * (nn(far_of(x, r2, 1, h), grad) - delta)).astype(BF16)
            query_part = query_part + tn(far_of(x, r2, 0, h), slope)
            bufs[1, part, cols(h)] = (query_part.T * SCALE).astype(BF16)
        bufs[2, :, cols(h)] = (kacc[...] * SCALE).astype(BF16)
        bufs[3, :, cols(h)] = vacc[...].astype(BF16)
        for i, out in enumerate((output, query_grad, key_grad, value_grad)):
            copies.append(
                pltpu.make_async_copy(
                    bufs.at[i, :, cols(h)], out.at[:, cols(h)], sems.at[h, i]
                )
            )
            copies[-1].start()
        for t in range(PICK):
            rows = pl.ds(pl.multiple_of(t * DILATION + group * 8, 8), 8)
            tiles[0, t, :, cols(h)] = kacc[rows, :] * SCALE
            tiles[1, t, :, cols(h)] = vacc[rows, :]
    for copy in copies:
        copy.wait()


def gather_kernel(ids, x, r2_part, own, back1, back2):
    z = ids[0] & 7
    for kv in range(2):
        a = jnp.zeros((PICK, WIDE), F32)
        b = jnp.zeros((PICK, WIDE), F32)
        c = r2_part[kv]
        for d in range(ZN):
            up = d >= z
            at = BACK_ORDER.index(d)
            low = x[at, kv, 0:PICK].astype(F32)
            high = x[at, kv, PICK : 2 * PICK].astype(F32)
            a = a + jnp.where(up, low, 0.0)
            b = b + jnp.where(up, high, low)
            c = c + jnp.where(up, 0.0, high)
        own[kv] = a
        back1[kv] = b.astype(BF16)
        back2[kv] = c.astype(BF16)


def finish_kernel(
    ids, own, back1, back2, tiles, _key, _value, key_grad, value_grad, kbuf, vbuf, sems
):
    group = lax.shift_right_logical(ids[1] * HEADS, 3)
    first = (ids[1] * HEADS) & 7
    inner = lax.broadcasted_iota(jnp.int32, (PICK, 8, D), 1)
    copies = []
    for kv, buf, out in ((0, kbuf, key_grad), (1, vbuf, value_grad)):
        for h in range(HEADS):
            far = (
                own[kv, :, cols(h)]
                + back1[kv, :, cols(h)].astype(F32)
                + back2[kv, :, cols(h)].astype(F32)
            )
            wide = jnp.where(inner == first + h, far[:, None, :], 0.0)
            buf[:, :, cols(h)] = (tiles[kv, :, :, cols(h)] + wide).astype(BF16)
        copies.append(pltpu.make_async_copy(buf, out.at[:, group], sems.at[kv]))
        copies[-1].start()
    for copy in copies:
        copy.wait()


SMEM = pl.BlockSpec(memory_space=pltpu.SMEM)
VMEM = pl.BlockSpec(memory_space=pltpu.VMEM)


ANY = pl.BlockSpec(memory_space=pltpu.HBM)


def call(kernel, specs, args, outs, scratch=(), flops=0, nbytes=0, out_specs=None, alias=None):
    specs = list(specs) + [VMEM] * (len(args) - len(specs))
    args = [
        pltpu.with_memory_space_constraint(a, pltpu.HBM) if s is ANY else a
        for a, s in zip(args, specs)
    ]
    return pl.pallas_call(
        kernel,
        out_shape=tuple(jax.ShapeDtypeStruct(s, t) for s, t in outs),
        in_specs=specs,
        out_specs=tuple(out_specs or [VMEM] * len(outs)),
        scratch_shapes=scratch,
        input_output_aliases=alias or {},
        compiler_params=pltpu.CompilerParams(vmem_limit_bytes=LIMIT),
        cost_estimate=pl.CostEstimate(flops=flops, bytes_accessed=nbytes, transcendentals=0),
    )(*args)


def along_y(step):
    return [(y * ZN + z, (y + step) % YN * ZN + z) for y in range(YN) for z in range(ZN)]


Z_OUT = [[y * ZN + z for z in OUT_ORDER] for y in range(YN)]
Z_BACK = [[y * ZN + z for z in BACK_ORDER] for y in range(YN)]


def along_x(step):
    return [(p, (p + 2 * step) % 8) for p in range(8)]


def shards(queries, keys, values, out_grad, norm_gain, doc_lengths, group_level):
    two = jnp.arange(2, dtype=jnp.int32)
    ids = jnp.where(two == 0, lax.axis_index("ctx"), lax.axis_index("head")).astype(jnp.int32)
    gain = norm_gain.reshape(1, WIDE)
    bundle = (2, PICK, WIDE)
    block = (ZN, 2, 2 * PICK, WIDE)
    square = (TOK, WIDE)
    tiled = (PICK, DILATION // 8, 8, WIDE)
    tile = (PICK, 8, WIDE)

    (mine,) = call(
        pick_kernel,
        [SMEM, ANY, ANY],
        (ids, keys.reshape(tiled), values.reshape(tiled)),
        [(bundle, BF16)],
        scratch=[pltpu.VMEM(tile, BF16), pltpu.VMEM(tile, BF16), pltpu.SemaphoreType.DMA((2,))],
        nbytes=1 << 18,
    )
    r1 = lax.ppermute(mine, "ctx", along_y(1))
    r2 = lax.ppermute(mine, "ctx", along_y(2))
    acc, rows, scaled, fbias, nbias, q, k, v, gain = call(
        near_forward_kernel,
        [SMEM] + [ANY] * 7,
        (ids, doc_lengths, group_level, queries, keys, values, out_grad, gain),
        [
            ((WIDE, TOK), F32), ((16, TOK), F32), ((WIDE, TOK), F32), ((HEADS, FAR, TOK), F32),
            ((TOK, TOK), F32), (square, BF16), (square, BF16), (square, BF16), ((1, WIDE), F32),
        ],
        scratch=[
            pltpu.VMEM(square, BF16), pltpu.SMEM((DOCS,), jnp.int32), pltpu.SMEM((8,), jnp.int32),
            pltpu.SemaphoreType.DMA((7,)),
        ],
        flops=4 * 4 * TOK * TOK * D,
        nbytes=4 << 20,
    )
    if NEAR_FIRST:
        r1, r2, acc = lax.optimization_barrier((r1, r2, acc))
    (sent,) = call(bundle_kernel, [SMEM], (ids, mine, r1, r2), [(block, BF16)], nbytes=1 << 19)
    x = lax.all_to_all(sent, "ctx", 0, 0, axis_index_groups=Z_OUT, tiled=True)
    flat, stats, totals = call(
        far_forward_kernel,
        [],
        (x, r2, q, acc, rows, scaled, fbias),
        [((WIDE, TOK), BF16), ((8, TOK), F32), ((8, TOK), F32)],
        flops=4 * 4 * TOK * FAR * D,
        nbytes=4 << 20,
    )
    s0 = stats + lax.ppermute(stats, "head", [(p, p ^ 1) for p in range(8)])
    s1, s2, s3 = (lax.ppermute(s0, "head", along_x(k)) for k in (1, 2, 3))
    _, later = lax.optimization_barrier((s0, totals))
    far_weight, near_weight = call(
        weight_kernel,
        [],
        (x, r2, q, k, later, fbias, nbias),
        [((HEADS, FAR, TOK), F32), ((HEADS, TOK, TOK), F32)],
        flops=2 * 4 * TOK * FAR * D,
        nbytes=4 << 20,
    )
    back, back_own = call(
        far_backward_kernel,
        [],
        (s0, s1, s2, s3, x, r2, q, flat, scaled, far_weight),
        [(block, BF16), (bundle, F32)],
        scratch=[pltpu.VMEM((FAR, D), F32), pltpu.VMEM((FAR, D), F32)],
        flops=8 * 4 * TOK * FAR * D,
        nbytes=4 << 20,
    )
    arrived = lax.all_to_all(back, "ctx", 0, 0, axis_index_groups=Z_BACK, tiled=True)
    output, query_grad, key_grad, value_grad, tiles = call(
        near_backward_kernel,
        [SMEM],
        (ids, s0, s1, s2, s3, x, r2, q, k, v, flat, scaled, far_weight, near_weight, gain),
        [(square, BF16)] * 4 + [((2, *tile), F32)],
        scratch=[
            pltpu.VMEM((TOK, D), F32), pltpu.VMEM((TOK, D), F32), pltpu.VMEM((4, *square), BF16),
            pltpu.SemaphoreType.DMA((HEADS, 4)),
        ],
        out_specs=[ANY] * 4 + [VMEM],
        flops=16 * 4 * TOK * TOK * D,
        nbytes=8 << 20,
    )
    if BACK_FIRST:
        arrived, tiles = lax.optimization_barrier((arrived, tiles))
    own, back1, back2 = call(
        gather_kernel,
        [SMEM],
        (ids, arrived, back_own),
        [(bundle, F32), (bundle, BF16), (bundle, BF16)],
        nbytes=1 << 20,
    )
    back1 = lax.ppermute(back1, "ctx", along_y(-1))
    back2 = lax.ppermute(back2, "ctx", along_y(-2))
    key_grad, value_grad = call(
        finish_kernel,
        [SMEM, VMEM, VMEM, VMEM, VMEM, ANY, ANY],
        (ids, own, back1, back2, tiles, key_grad.reshape(tiled), value_grad.reshape(tiled)),
        [(tiled, BF16), (tiled, BF16)],
        scratch=[pltpu.VMEM(tile, BF16), pltpu.VMEM(tile, BF16), pltpu.SemaphoreType.DMA((2,))],
        out_specs=[ANY, ANY],
        alias={5: 0, 6: 1},
        nbytes=1 << 18,
    )
    return output, query_grad, key_grad.reshape(square), value_grad.reshape(square)


def solution(mesh):
    tokens = P("ctx", "head")
    return jax.shard_map(
        shards,
        mesh=mesh,
        in_specs=(tokens, tokens, tokens, tokens, P("head"), P(), P()),
        out_specs=(tokens, tokens, tokens, tokens),
        check_vma=False,
    )
```

```python
import functools

import jax
import jax.numpy as jnp
from jax import lax
from jax.experimental import pallas as pl
from jax.experimental.pallas import tpu as pltpu
from jax.sharding import PartitionSpec as P

D = 128
HEADS = 4
TOK = 512
WIDE = HEADS * D
DILATION = 32
DOCS = 16
PICK = TOK // DILATION
ZN = 8
YN = 4
FAR = 17 * PICK
HALF = 256
FULL = 4096.0
EPS = 1e-05
SCALE = D ** (-0.5)
C2 = SCALE * 1.4426950408889634
NEG = -1e30
LIMIT = 8 << 20
SHIFTS = (4, 3, 5, 2, 6, 1, 7)
BACK_SHIFTS = (4, 3, 5, 2, 6, 1, 7)


F32 = jnp.float32
BF16 = jnp.bfloat16


def nn(a, b):
    return lax.dot_general(a, b, (((1,), (0,)), ((), ())), preferred_element_type=F32)


def nt(a, b):
    return lax.dot_general(a, b, (((1,), (1,)), ((), ())), preferred_element_type=F32)


def tn(a, b):
    return lax.dot_general(a, b, (((0,), (0,)), ((), ())), preferred_element_type=F32)


EARLY, LATE = (0, 1), (2, 3)


def cols(h):
    return slice(h * D, (h + 1) * D)


def query_rows(ids, lens):
    place = ids[0] * TOK + lax.broadcasted_iota(jnp.int32, (1, TOK), 1)
    start = jnp.zeros((1, TOK), jnp.int32)
    end = jnp.int32(0)
    for k in range(DOCS):
        end = end + lens[k]
        start = jnp.where(place >= end, end, start)
    return place, start


def near_bias(place, start, at, depth):
    base = place[:, 0:1]
    key = lax.broadcasted_iota(jnp.int32, (depth, HALF), 0)
    query = place[:, at : at + HALF] - base
    first = start[:, at : at + HALF] - base
    return jnp.where((key <= query) & (key >= first), 0.0, NEG)


def far_places(ids, levels):
    row = lax.broadcasted_iota(jnp.int32, (FAR, 1), 0)
    block = lax.shift_right_logical(row, 4)
    t = row & 15
    z = ids[0] & 7
    y = lax.shift_right_logical(ids[0], 3)
    pair = lax.shift_right_logical(block, 1)
    shift = jnp.zeros_like(pair)
    for i, k in enumerate(SHIFTS):
        shift = jnp.where(pair == i, k, shift)
    from_z = (z - shift) & 7
    at = (y - (block & 1) - jnp.where(from_z > z, 1, 0)) * ZN + from_z
    at = jnp.where(block >= 14, (y - (block - 14)) * ZN + z, at)
    rate = lax.shift_left(jnp.int32(1), levels[ids[1]])
    return jnp.where((t & (rate - 1)) == 0, at * TOK + t * DILATION, -(1 << 29))


def pick_kernel(ids, k, v, out, kbuf, vbuf, sems):
    group = lax.shift_right_logical(ids[1] * HEADS, 3)
    copies = [
        pltpu.make_async_copy(k.at[:, group], kbuf, sems.at[0]),
        pltpu.make_async_copy(v.at[:, group], vbuf, sems.at[1]),
    ]
    for copy in copies:
        copy.start()
    row = lax.broadcasted_iota(jnp.int32, (PICK, PICK * 8), 0) * 8
    col = lax.broadcasted_iota(jnp.int32, (PICK, PICK * 8), 1)
    first = (ids[1] * HEADS) & 7
    for kv, buf in enumerate((kbuf, vbuf)):
        copies[kv].wait()
        for h in range(HEADS):
            one = jnp.where(col == row + (first + h), 1.0, 0.0).astype(BF16)
            rows = buf[:, :, cols(h)].astype(F32).reshape(PICK * 8, D).astype(BF16)
            out[kv, :, cols(h)] = nn(one, rows).astype(BF16)


def bundle_kernel(ids, own, r1, r2, *outs):
    z = ids[0] & 7
    for k, out in zip(SHIFTS, outs):
        up = z + k < ZN
        out[:, 0:PICK] = jnp.where(up, own[...], r1[...])
        out[:, PICK : 2 * PICK] = jnp.where(up, r1[...], r2[...])


def prepare_kernel(
    ids, lens_at, levels_at, q_at, k_at, v_at, g_at, gain_at,
    scaled, fbias, nbias, grads, q, k, v, gain, g, lens, levels, sems,
):
    pairs = (
        (lens_at, lens), (levels_at, levels), (g_at, g), (gain_at, gain), (q_at, q), (k_at, k),
        (v_at, v),
    )
    copies = [pltpu.make_async_copy(a, b, sems.at[i]) for i, (a, b) in enumerate(pairs)]
    for copy in copies:
        copy.start()
    for copy in copies[:2]:
        copy.wait()
    place, start = query_rows(ids, lens)
    fplace = far_places(ids, levels)
    for h in range(HEADS):
        offset = ids[1] * HEADS + h
        live = (fplace <= place - offset) & (fplace >= start - offset)
        fbias[h] = jnp.where(live, 0.0, NEG)
    for at in range(0, TOK, HALF):
        nbias[: at + HALF, at : at + HALF] = near_bias(place, start, at, at + HALF)
    nbias[HALF:, :HALF] = jnp.full((HALF, HALF), NEG, F32)
    for copy in copies[2:4]:
        copy.wait()
    total = jnp.zeros((1, TOK), F32)
    for h in range(HEADS):
        part = (g[:, cols(h)].astype(F32) * gain[:, cols(h)]).T
        scaled[cols(h), :] = part
        total = total + jnp.sum(part, axis=0, keepdims=True)
    grads[0:1, :] = total
    grads[1:8, :] = jnp.zeros((7, TOK), F32)
    for copy in copies[4:]:
        copy.wait()


def near_forward_kernel(ids, nbias, grads, q, k, v, acc, rows):
    for h in range(HEADS):
        for at in range(0, TOK, HALF):
            depth = at + HALF
            s = nt(k[:depth, cols(h)], q[at:depth, cols(h)]) * C2 + nbias[:depth, at:depth]
            top = jnp.max(s, axis=0, keepdims=True)
            p = jnp.exp2(s - top)
            rows[h : h + 1, at:depth] = top
            rows[HEADS + h : HEADS + h + 1, at:depth] = jnp.sum(p, axis=0, keepdims=True)
            acc[cols(h), at:depth] = tn(v[:depth, cols(h)], p.astype(BF16))
    rows[8:16, :] = grads[...]


def far_forward_kernel(*refs):
    from_z, refs = refs[:7], refs[7:]
    own, r1, r2, q, acc, rows, scaled, fbias, flat, stats, totals, fk, fv = refs
    for kv, out in ((0, fk), (1, fv)):
        for i, a in enumerate(from_z):
            out[i * 2 * PICK : (i + 1) * 2 * PICK, :] = a[kv]
        for i, a in enumerate((own, r1, r2)):
            out[14 * PICK + i * PICK : 15 * PICK + i * PICK, :] = a[kv]
    for at in range(0, TOK, HALF):
        part = slice(at, at + HALF)
        sums = jnp.zeros((1, HALF), F32)
        squares = jnp.zeros((1, HALF), F32)
        cross = jnp.zeros((1, HALF), F32)
        for h in range(HEADS):
            s = nt(fk[:, cols(h)], q[part, cols(h)]) * C2 + fbias[h, :, part]
            near_top = rows[h : h + 1, part]
            top = jnp.maximum(near_top, jnp.max(s, axis=0, keepdims=True))
            p = jnp.exp2(s - top)
            shrink = jnp.exp2(near_top - top)
            total = rows[HEADS + h : HEADS + h + 1, part] * shrink + jnp.sum(
                p, axis=0, keepdims=True
            )
            o = acc[cols(h), part] * shrink + tn(fv[:, cols(h)], p.astype(BF16))
            o = (o * (1.0 / total)).astype(BF16)
            flat[cols(h), part] = o
            totals[h : h + 1, part] = top + jnp.log2(total)
            f = o.astype(F32)
            sums = sums + jnp.sum(f, axis=0, keepdims=True)
            squares = squares + jnp.sum(f * f, axis=0, keepdims=True)
            cross = cross + jnp.sum(f * scaled[cols(h), part], axis=0, keepdims=True)
        stats[0:1, part] = sums
        stats[1:2, part] = squares
        stats[2:3, part] = rows[8:9, part]
        stats[3:4, part] = cross
    stats[4:8, :] = jnp.zeros((4, TOK), F32)
    totals[4:8, :] = jnp.zeros((4, TOK), F32)


def weight_kernel(far_keys, q, k, totals, fbias, nbias, far_weight, near_weight):
    for h in range(HEADS):
        fk = far_keys[:, cols(h)]
        for at in range(0, TOK, HALF):
            depth = at + HALF
            total = totals[h : h + 1, at:depth]
            qh = q[at:depth, cols(h)]
            far_weight[h, :, at:depth] = jnp.exp2(nt(fk, qh) * C2 + fbias[h, :, at:depth] - total)
            near_weight[h, :depth, at:depth] = jnp.exp2(
                nt(k[:depth, cols(h)], qh) * C2 + nbias[:depth, at:depth] - total
            )


def norm_rows(s0, s1, s2, s3, part):
    tot = (s0[:, part] + s1[:, part]) + (s2[:, part] + s3[:, part])
    mean = tot[0:1] / FULL
    rstd = lax.rsqrt(tot[1:2] / FULL - mean * mean + EPS)
    grad_mean = tot[2:3] / FULL
    grad_proj = rstd * (tot[3:4] - mean * tot[2:3]) / FULL
    return mean, rstd, grad_mean, grad_proj


def att_grad_of(flat, scaled, norm, h, part):
    mean, rstd, grad_mean, grad_proj = norm
    f = flat[cols(h), part].astype(F32)
    normed = (f - mean) * rstd
    grad = (rstd * (scaled[cols(h), part] - grad_mean - normed * grad_proj)).astype(BF16)
    delta = jnp.sum(grad.astype(F32) * f, axis=0, keepdims=True)
    return grad, delta, normed


def far_backward_kernel(s0, s1, s2, s3, fv, q, flat, scaled, weight, *refs):
    outs, (own, kacc, vacc) = refs[:7], refs[7:]
    for h in range(HEADS):
        key_part = jnp.zeros((FAR, D), F32)
        value_part = jnp.zeros((FAR, D), F32)
        for at in range(0, TOK, HALF):
            part = slice(at, at + HALF)
            norm = norm_rows(s0, s1, s2, s3, part)
            grad, delta, _ = att_grad_of(flat, scaled, norm, h, part)
            p = weight[h, :, part]
            slope = (p * (nn(fv[:, cols(h)], grad) - delta)).astype(BF16)
            key_part = key_part + nn(slope, q[part, cols(h)])
            value_part = value_part + nt(p.astype(BF16), grad)
        kacc[...] = key_part * SCALE
        vacc[...] = value_part
        for kv, grads in ((0, kacc), (1, vacc)):
            for i, out in enumerate(outs):
                out[kv, :, cols(h)] = grads[i * 2 * PICK : (i + 1) * 2 * PICK, :].astype(BF16)
            for i in range(3):
                own[i, kv, :, cols(h)] = grads[(14 + i) * PICK : (15 + i) * PICK, :]


def near_backward_kernel(heads, ids, *refs):
    s0, s1, s2, s3, fk, fv, q, k, v, flat, scaled, far_weight, near_weight, gain = refs[:14]
    outs, (tiles, kacc, vacc, bufs, sems) = refs[-9:-5], refs[-5:]
    group = lax.shift_right_logical(ids[1] * HEADS, 3)
    norms = [norm_rows(s0, s1, s2, s3, slice(at, at + HALF)) for at in range(0, TOK, HALF)]
    copies = []
    for i, h in enumerate(heads):
        here = cols(i)
        for at in range(0, TOK, HALF):
            part = slice(at, at + HALF)
            depth = at + HALF
            grad, delta, normed = att_grad_of(flat, scaled, norms[at // HALF], h, part)
            bufs[0, part, here] = (normed.T * gain[:, cols(h)]).astype(BF16)
            qh = q[part, cols(h)]
            kh, vh = k[:depth, cols(h)], v[:depth, cols(h)]
            p = near_weight[h, :depth, part]
            slope = (p * (nn(vh, grad) - delta)).astype(BF16)
            key_part = nn(slope, qh)
            value_part = nt(p.astype(BF16), grad)
            if at == 0:
                kacc[:depth, :] = key_part
                vacc[:depth, :] = value_part
            else:
                kacc[:at, :] += key_part[:at]
                vacc[:at, :] += value_part[:at]
                kacc[at:, :] = key_part[at:]
                vacc[at:, :] = value_part[at:]
            query_part = tn(kh, slope)
            slope = (far_weight[h, :, part] * (nn(fv[:, cols(h)], grad) - delta)).astype(BF16)
            query_part = query_part + tn(fk[:, cols(h)], slope)
            bufs[1, part, here] = (query_part.T * SCALE).astype(BF16)
        bufs[2, :, here] = (kacc[...] * SCALE).astype(BF16)
        bufs[3, :, here] = vacc[...].astype(BF16)
        for n, out in enumerate(outs):
            copies.append(
                pltpu.make_async_copy(bufs.at[n, :, here], out.at[:, cols(h)], sems.at[i, n])
            )
            copies[-1].start()
        for t in range(PICK):
            rows = pl.ds(pl.multiple_of(t * DILATION + group * 8, 8), 8)
            tiles[0, t, :, here] = kacc[rows, :] * SCALE
            tiles[1, t, :, here] = vacc[rows, :]
    for copy in copies:
        copy.wait()


def gather_kernel(ids, mine, *refs):
    from_z, (own, back1, back2) = refs[:7], refs[7:]
    z = ids[0] & 7
    for kv in range(2):
        a, b, c = mine[0, kv], mine[1, kv], mine[2, kv]
        for k, part in zip(SHIFTS, from_z):
            up = z + k < ZN
            low = part[kv, 0:PICK].astype(F32)
            high = part[kv, PICK : 2 * PICK].astype(F32)
            a = a + jnp.where(up, low, 0.0)
            b = b + jnp.where(up, high, low)
            c = c + jnp.where(up, 0.0, high)
        own[kv] = a
        back1[kv] = b.astype(BF16)
        back2[kv] = c.astype(BF16)


def finish_kernel(
    ids, own, back1, back2, early, late, _key, _value, key_grad, value_grad, kbuf, vbuf, sems
):
    group = lax.shift_right_logical(ids[1] * HEADS, 3)
    first = (ids[1] * HEADS) & 7
    inner = lax.broadcasted_iota(jnp.int32, (PICK, 8, D), 1)
    copies = []
    for kv, buf, out in ((0, kbuf, key_grad), (1, vbuf, value_grad)):
        for h in range(HEADS):
            far = (
                own[kv, :, cols(h)]
                + back1[kv, :, cols(h)].astype(F32)
                + back2[kv, :, cols(h)].astype(F32)
            )
            wide = jnp.where(inner == first + h, far[:, None, :], 0.0)
            near = (early if h in EARLY else late)[kv, :, :, cols(h % 2)]
            buf[:, :, cols(h)] = (near + wide).astype(BF16)
        copies.append(pltpu.make_async_copy(buf, out.at[:, group], sems.at[kv]))
        copies[-1].start()
    for copy in copies:
        copy.wait()


SMEM = pl.BlockSpec(memory_space=pltpu.SMEM)
VMEM = pl.BlockSpec(memory_space=pltpu.VMEM)


ANY = pl.BlockSpec(memory_space=pltpu.HBM)


def call(kernel, specs, args, outs, scratch=(), flops=0, nbytes=0, out_specs=None, alias=None):
    specs = list(specs) + [VMEM] * (len(args) - len(specs))
    args = [
        pltpu.with_memory_space_constraint(a, pltpu.HBM) if s is ANY else a
        for a, s in zip(args, specs)
    ]
    return pl.pallas_call(
        kernel,
        out_shape=tuple(jax.ShapeDtypeStruct(s, t) for s, t in outs),
        in_specs=specs,
        out_specs=tuple(out_specs or [VMEM] * len(outs)),
        scratch_shapes=scratch,
        input_output_aliases=alias or {},
        compiler_params=pltpu.CompilerParams(vmem_limit_bytes=LIMIT),
        cost_estimate=pl.CostEstimate(flops=flops, bytes_accessed=nbytes, transcendentals=0),
    )(*args)


def along_y(step):
    return [(y * ZN + z, (y + step) % YN * ZN + z) for y in range(YN) for z in range(ZN)]


def along_z(step):
    return [(y * ZN + z, y * ZN + (z + step) % ZN) for y in range(YN) for z in range(ZN)]


def along_x(step):
    return [(p, (p + 2 * step) % 8) for p in range(8)]


def shards(queries, keys, values, out_grad, norm_gain, doc_lengths, group_level):
    two = jnp.arange(2, dtype=jnp.int32)
    ids = jnp.where(two == 0, lax.axis_index("ctx"), lax.axis_index("head")).astype(jnp.int32)
    gain = norm_gain.reshape(1, WIDE)
    bundle = (2, PICK, WIDE)
    column = (2, 2 * PICK, WIDE)
    square = (TOK, WIDE)
    tiled = (PICK, DILATION // 8, 8, WIDE)
    tile = (PICK, 8, WIDE)

    (mine,) = call(
        pick_kernel,
        [SMEM, ANY, ANY],
        (ids, keys.reshape(tiled), values.reshape(tiled)),
        [(bundle, BF16)],
        scratch=[pltpu.VMEM(tile, BF16), pltpu.VMEM(tile, BF16), pltpu.SemaphoreType.DMA((2,))],
        nbytes=1 << 18,
    )
    r1 = lax.ppermute(mine, "ctx", along_y(1))
    r2 = lax.ppermute(mine, "ctx", along_y(2))
    scaled, fbias, nbias, grads, q, k, v, gain = call(
        prepare_kernel,
        [SMEM] + [ANY] * 7,
        (ids, doc_lengths, group_level, queries, keys, values, out_grad, gain),
        [
            ((WIDE, TOK), F32), ((HEADS, FAR, TOK), F32), ((TOK, TOK), F32), ((8, TOK), F32),
            (square, BF16), (square, BF16), (square, BF16), ((1, WIDE), F32),
        ],
        scratch=[
            pltpu.VMEM(square, BF16), pltpu.SMEM((DOCS,), jnp.int32), pltpu.SMEM((8,), jnp.int32),
            pltpu.SemaphoreType.DMA((7,)),
        ],
        flops=4 * TOK * TOK * D,
        nbytes=4 << 20,
    )
    r1, r2, nbias = lax.optimization_barrier((r1, r2, nbias))
    sent = call(
        bundle_kernel, [SMEM], (ids, mine, r1, r2), [(column, BF16)] * 7, nbytes=1 << 19
    )
    got = [lax.ppermute(a, "ctx", along_z(k)) for k, a in zip(SHIFTS, sent)]
    *_, later_ids = lax.optimization_barrier((*sent, ids))
    acc, rows = call(
        near_forward_kernel,
        [SMEM],
        (later_ids, nbias, grads, q, k, v),
        [((WIDE, TOK), F32), ((16, TOK), F32)],
        flops=4 * 4 * TOK * TOK * D,
        nbytes=4 << 20,
    )
    flat, stats, totals, fk, fv = call(
        far_forward_kernel,
        [],
        (*got, mine, r1, r2, q, acc, rows, scaled, fbias),
        [
            ((WIDE, TOK), BF16), ((8, TOK), F32), ((8, TOK), F32),
            ((FAR, WIDE), BF16), ((FAR, WIDE), BF16),
        ],
        flops=4 * 4 * TOK * FAR * D,
        nbytes=4 << 20,
    )
    s0 = stats + lax.ppermute(stats, "head", [(p, p ^ 1) for p in range(8)])
    s1, s2, s3 = (lax.ppermute(s0, "head", along_x(k)) for k in (1, 2, 3))
    _, later = lax.optimization_barrier((s0, totals))
    far_weight, near_weight = call(
        weight_kernel,
        [],
        (fk, q, k, later, fbias, nbias),
        [((HEADS, FAR, TOK), F32), ((HEADS, TOK, TOK), F32)],
        flops=2 * 4 * TOK * FAR * D,
        nbytes=4 << 20,
    )
    *back, back_own = call(
        far_backward_kernel,
        [],
        (s0, s1, s2, s3, fv, q, flat, scaled, far_weight),
        [(column, BF16)] * 7 + [((3, *bundle), F32)],
        scratch=[pltpu.VMEM((FAR, D), F32), pltpu.VMEM((FAR, D), F32)],
        flops=8 * 4 * TOK * FAR * D,
        nbytes=4 << 20,
    )
    to_send = dict(zip(SHIFTS, back))
    home = {k: lax.ppermute(to_send[k], "ctx", along_z(-k)) for k in BACK_SHIFTS}
    arrived = [home[k] for k in SHIFTS]
    *_, later_ids = lax.optimization_barrier((*back, ids))
    operands = (s0, s1, s2, s3, fk, fv, q, k, v, flat, scaled, far_weight, near_weight, gain)
    near_scratch = [
        pltpu.VMEM((TOK, D), F32), pltpu.VMEM((TOK, D), F32),
        pltpu.VMEM((4, TOK, 2 * D), BF16), pltpu.SemaphoreType.DMA((2, 4)),
    ]
    halves = [(square, BF16)] * 4 + [((2, PICK, 8, 2 * D), F32)]
    *partial, early = call(
        functools.partial(near_backward_kernel, EARLY),
        [SMEM],
        (later_ids, *operands),
        halves,
        scratch=near_scratch,
        out_specs=[ANY] * 4 + [VMEM],
        flops=8 * 4 * TOK * TOK * D,
        nbytes=4 << 20,
    )
    *arrived, early = lax.optimization_barrier((*arrived, early))
    own, back1, back2 = call(
        gather_kernel,
        [SMEM],
        (ids, back_own, *arrived),
        [(bundle, F32), (bundle, BF16), (bundle, BF16)],
        nbytes=1 << 20,
    )
    _, later_ids = lax.optimization_barrier((back1, ids))
    back1 = lax.ppermute(back1, "ctx", along_y(-1))
    back2 = lax.ppermute(back2, "ctx", along_y(-2))
    output, query_grad, key_grad, value_grad, late = call(
        functools.partial(near_backward_kernel, LATE),
        [SMEM] + [VMEM] * 14 + [ANY] * 4,
        (later_ids, *operands, *partial),
        halves,
        scratch=near_scratch,
        out_specs=[ANY] * 4 + [VMEM],
        alias={15: 0, 16: 1, 17: 2, 18: 3},
        flops=8 * 4 * TOK * TOK * D,
        nbytes=4 << 20,
    )
    key_grad, value_grad = call(
        finish_kernel,
        [SMEM, VMEM, VMEM, VMEM, VMEM, VMEM, ANY, ANY],
        (ids, own, back1, back2, early, late, key_grad.reshape(tiled), value_grad.reshape(tiled)),
        [(tiled, BF16), (tiled, BF16)],
        scratch=[pltpu.VMEM(tile, BF16), pltpu.VMEM(tile, BF16), pltpu.SemaphoreType.DMA((2,))],
        out_specs=[ANY, ANY],
        alias={6: 0, 7: 1},
        nbytes=1 << 18,
    )
    return output, query_grad, key_grad.reshape(square), value_grad.reshape(square)


def solution(mesh):
    tokens = P("ctx", "head")
    return jax.shard_map(
        shards,
        mesh=mesh,
        in_specs=(tokens, tokens, tokens, tokens, P("head"), P(), P()),
        out_specs=(tokens, tokens, tokens, tokens),
        check_vma=False,
    )
```

```python
import functools

import jax
import jax.numpy as jnp
from jax import lax
from jax.experimental import pallas as pl
from jax.experimental.pallas import tpu as pltpu
from jax.sharding import PartitionSpec as P

D = 128
HEADS = 4
TOK = 512
WIDE = HEADS * D
DILATION = 32
DOCS = 16
PICK = TOK // DILATION
ZN = 8
YN = 4
FAR = 17 * PICK
HALF = 256
SPAN = 512
FULL = 4096.0
EPS = 1e-05
SCALE = D ** (-0.5)
C2 = SCALE * 1.4426950408889634
NEG = -1e30
LIMIT = 8 << 20
SHIFTS = (4, 3, 5, 2, 6, 1, 7)
BACK_SHIFTS = (4, 3, 5, 2, 6, 1, 7)


F32 = jnp.float32
BF16 = jnp.bfloat16


def nn(a, b):
    return lax.dot_general(a, b, (((1,), (0,)), ((), ())), preferred_element_type=F32)


def nt(a, b):
    return lax.dot_general(a, b, (((1,), (1,)), ((), ())), preferred_element_type=F32)


def tn(a, b):
    return lax.dot_general(a, b, (((0,), (0,)), ((), ())), preferred_element_type=F32)


EARLY, LATE = (0, 1), (2, 3)


def cols(h):
    return slice(h * D, (h + 1) * D)


def query_rows(ids, lens):
    place = ids[0] * TOK + lax.broadcasted_iota(jnp.int32, (1, TOK), 1)
    start = jnp.zeros((1, TOK), jnp.int32)
    end = jnp.int32(0)
    for k in range(DOCS):
        end = end + lens[k]
        start = jnp.where(place >= end, end, start)
    return place, start


def near_bias(place, start, at, depth):
    base = place[:, 0:1]
    key = lax.broadcasted_iota(jnp.int32, (depth, HALF), 0)
    query = place[:, at : at + HALF] - base
    first = start[:, at : at + HALF] - base
    return jnp.where((key <= query) & (key >= first), 0.0, NEG)


def far_places(ids, levels):
    row = lax.broadcasted_iota(jnp.int32, (FAR, 1), 0)
    block = lax.shift_right_logical(row, 4)
    t = row & 15
    z = ids[0] & 7
    y = lax.shift_right_logical(ids[0], 3)
    pair = lax.shift_right_logical(block, 1)
    shift = jnp.zeros_like(pair)
    for i, k in enumerate(SHIFTS):
        shift = jnp.where(pair == i, k, shift)
    from_z = (z - shift) & 7
    at = (y - (block & 1) - jnp.where(from_z > z, 1, 0)) * ZN + from_z
    at = jnp.where(block >= 14, (y - (block - 14)) * ZN + z, at)
    rate = lax.shift_left(jnp.int32(1), levels[ids[1]])
    return jnp.where((t & (rate - 1)) == 0, at * TOK + t * DILATION, -(1 << 29))


def pick_kernel(ids, k, v, out, kbuf, vbuf, sems):
    group = lax.shift_right_logical(ids[1] * HEADS, 3)
    copies = [
        pltpu.make_async_copy(k.at[:, group], kbuf, sems.at[0]),
        pltpu.make_async_copy(v.at[:, group], vbuf, sems.at[1]),
    ]
    for copy in copies:
        copy.start()
    row = lax.broadcasted_iota(jnp.int32, (PICK, PICK * 8), 0) * 8
    col = lax.broadcasted_iota(jnp.int32, (PICK, PICK * 8), 1)
    first = (ids[1] * HEADS) & 7
    for kv, buf in enumerate((kbuf, vbuf)):
        copies[kv].wait()
        for h in range(HEADS):
            one = jnp.where(col == row + (first + h), 1.0, 0.0).astype(BF16)
            rows = buf[:, :, cols(h)].astype(F32).reshape(PICK * 8, D).astype(BF16)
            out[kv, :, cols(h)] = nn(one, rows).astype(BF16)


def bundle_kernel(ids, own, r1, r2, *outs):
    z = ids[0] & 7
    for k, out in zip(SHIFTS, outs):
        up = z + k < ZN
        out[:, 0:PICK] = jnp.where(up, own[...], r1[...])
        out[:, PICK : 2 * PICK] = jnp.where(up, r1[...], r2[...])


def prepare_kernel(
    ids, lens_at, levels_at, q_at, k_at, v_at, g_at, gain_at,
    scaled, fbias, nbias, grads, q, k, v, gain, g, lens, levels, sems,
):
    pairs = (
        (lens_at, lens), (levels_at, levels), (g_at, g), (gain_at, gain), (q_at, q), (k_at, k),
        (v_at, v),
    )
    copies = [pltpu.make_async_copy(a, b, sems.at[i]) for i, (a, b) in enumerate(pairs)]
    for copy in copies:
        copy.start()
    for copy in copies[:2]:
        copy.wait()
    place, start = query_rows(ids, lens)
    fplace = far_places(ids, levels)
    for h in range(HEADS):
        offset = ids[1] * HEADS + h
        live = (fplace <= place - offset) & (fplace >= start - offset)
        fbias[h] = jnp.where(live, 0.0, NEG)
    for at in range(0, TOK, HALF):
        nbias[: at + HALF, at : at + HALF] = near_bias(place, start, at, at + HALF)
    nbias[HALF:, :HALF] = jnp.full((HALF, HALF), NEG, F32)
    for copy in copies[2:4]:
        copy.wait()
    total = jnp.zeros((1, TOK), F32)
    for h in range(HEADS):
        part = (g[:, cols(h)].astype(F32) * gain[:, cols(h)]).T
        scaled[cols(h), :] = part
        total = total + jnp.sum(part, axis=0, keepdims=True)
    grads[0:1, :] = total
    grads[1:8, :] = jnp.zeros((7, TOK), F32)
    for copy in copies[4:]:
        copy.wait()


def near_forward_kernel(ids, nbias, grads, q, k, v, acc, rows):
    for h in range(HEADS):
        for at in range(0, TOK, HALF):
            depth = at + HALF
            s = nt(k[:depth, cols(h)], q[at:depth, cols(h)]) * C2 + nbias[:depth, at:depth]
            top = jnp.max(s, axis=0, keepdims=True)
            p = jnp.exp2(s - top)
            rows[h : h + 1, at:depth] = top
            rows[HEADS + h : HEADS + h + 1, at:depth] = jnp.sum(p, axis=0, keepdims=True)
            acc[cols(h), at:depth] = tn(v[:depth, cols(h)], p.astype(BF16))
    rows[8:16, :] = grads[...]


def far_forward_kernel(*refs):
    from_z, refs = refs[:7], refs[7:]
    own, r1, r2, q, acc, rows, scaled, fbias, flat, stats, totals, fk, fv = refs
    for kv, out in ((0, fk), (1, fv)):
        for i, a in enumerate(from_z):
            out[i * 2 * PICK : (i + 1) * 2 * PICK, :] = a[kv]
        for i, a in enumerate((own, r1, r2)):
            out[14 * PICK + i * PICK : 15 * PICK + i * PICK, :] = a[kv]
    for at in range(0, TOK, SPAN):
        part = slice(at, at + SPAN)
        sums = jnp.zeros((1, SPAN), F32)
        squares = jnp.zeros((1, SPAN), F32)
        cross = jnp.zeros((1, SPAN), F32)
        for h in range(HEADS):
            s = nt(fk[:, cols(h)], q[part, cols(h)]) * C2 + fbias[h, :, part]
            near_top = rows[h : h + 1, part]
            top = jnp.maximum(near_top, jnp.max(s, axis=0, keepdims=True))
            p = jnp.exp2(s - top)
            shrink = jnp.exp2(near_top - top)
            total = rows[HEADS + h : HEADS + h + 1, part] * shrink + jnp.sum(
                p, axis=0, keepdims=True
            )
            o = acc[cols(h), part] * shrink + tn(fv[:, cols(h)], p.astype(BF16))
            o = (o * (1.0 / total)).astype(BF16)
            flat[cols(h), part] = o
            totals[h : h + 1, part] = top + jnp.log2(total)
            f = o.astype(F32)
            sums = sums + jnp.sum(f, axis=0, keepdims=True)
            squares = squares + jnp.sum(f * f, axis=0, keepdims=True)
            cross = cross + jnp.sum(f * scaled[cols(h), part], axis=0, keepdims=True)
        stats[0:1, part] = sums
        stats[1:2, part] = squares
        stats[2:3, part] = rows[8:9, part]
        stats[3:4, part] = cross
    stats[4:8, :] = jnp.zeros((4, TOK), F32)
    totals[4:8, :] = jnp.zeros((4, TOK), F32)


def weight_kernel(far_keys, q, k, totals, fbias, nbias, far_weight, near_weight):
    for h in range(HEADS):
        fk = far_keys[:, cols(h)]
        for at in range(0, TOK, HALF):
            depth = at + HALF
            total = totals[h : h + 1, at:depth]
            qh = q[at:depth, cols(h)]
            far_weight[h, :, at:depth] = jnp.exp2(nt(fk, qh) * C2 + fbias[h, :, at:depth] - total)
            near_weight[h, :depth, at:depth] = jnp.exp2(
                nt(k[:depth, cols(h)], qh) * C2 + nbias[:depth, at:depth] - total
            )


def norm_rows(s0, s1, s2, s3, part):
    tot = (s0[:, part] + s1[:, part]) + (s2[:, part] + s3[:, part])
    mean = tot[0:1] / FULL
    rstd = lax.rsqrt(tot[1:2] / FULL - mean * mean + EPS)
    grad_mean = tot[2:3] / FULL
    grad_proj = rstd * (tot[3:4] - mean * tot[2:3]) / FULL
    return mean, rstd, grad_mean, grad_proj


def att_grad_of(flat, scaled, norm, h, part):
    mean, rstd, grad_mean, grad_proj = norm
    f = flat[cols(h), part].astype(F32)
    normed = (f - mean) * rstd
    grad = (rstd * (scaled[cols(h), part] - grad_mean - normed * grad_proj)).astype(BF16)
    delta = jnp.sum(grad.astype(F32) * f, axis=0, keepdims=True)
    return grad, delta, normed


def far_backward_kernel(s0, s1, s2, s3, fv, q, flat, scaled, weight, *refs):
    outs, (own, kacc, vacc) = refs[:7], refs[7:]
    for h in range(HEADS):
        key_part = jnp.zeros((FAR, D), F32)
        value_part = jnp.zeros((FAR, D), F32)
        for at in range(0, TOK, HALF):
            part = slice(at, at + HALF)
            norm = norm_rows(s0, s1, s2, s3, part)
            grad, delta, _ = att_grad_of(flat, scaled, norm, h, part)
            p = weight[h, :, part]
            slope = (p * (nn(fv[:, cols(h)], grad) - delta)).astype(BF16)
            key_part = key_part + nn(slope, q[part, cols(h)])
            value_part = value_part + nt(p.astype(BF16), grad)
        kacc[...] = key_part * SCALE
        vacc[...] = value_part
        for kv, grads in ((0, kacc), (1, vacc)):
            for i, out in enumerate(outs):
                out[kv, :, cols(h)] = grads[i * 2 * PICK : (i + 1) * 2 * PICK, :].astype(BF16)
            for i in range(3):
                own[i, kv, :, cols(h)] = grads[(14 + i) * PICK : (15 + i) * PICK, :]


def near_backward_kernel(heads, ids, *refs):
    s0, s1, s2, s3, fk, fv, q, k, v, flat, scaled, far_weight, near_weight, gain = refs[:14]
    outs, (tiles, kacc, vacc, bufs, sems) = refs[-9:-5], refs[-5:]
    group = lax.shift_right_logical(ids[1] * HEADS, 3)
    norms = [norm_rows(s0, s1, s2, s3, slice(at, at + HALF)) for at in range(0, TOK, HALF)]
    copies = []
    for i, h in enumerate(heads):
        here = cols(i)
        for at in range(0, TOK, HALF):
            part = slice(at, at + HALF)
            depth = at + HALF
            grad, delta, normed = att_grad_of(flat, scaled, norms[at // HALF], h, part)
            bufs[0, part, here] = (normed.T * gain[:, cols(h)]).astype(BF16)
            qh = q[part, cols(h)]
            kh, vh = k[:depth, cols(h)], v[:depth, cols(h)]
            p = near_weight[h, :depth, part]
            slope = (p * (nn(vh, grad) - delta)).astype(BF16)
            key_part = nn(slope, qh)
            value_part = nt(p.astype(BF16), grad)
            if at == 0:
                kacc[:depth, :] = key_part
                vacc[:depth, :] = value_part
            else:
                kacc[:at, :] += key_part[:at]
                vacc[:at, :] += value_part[:at]
                kacc[at:, :] = key_part[at:]
                vacc[at:, :] = value_part[at:]
            query_part = tn(kh, slope)
            slope = (far_weight[h, :, part] * (nn(fv[:, cols(h)], grad) - delta)).astype(BF16)
            query_part = query_part + tn(fk[:, cols(h)], slope)
            bufs[1, part, here] = (query_part.T * SCALE).astype(BF16)
        bufs[2, :, here] = (kacc[...] * SCALE).astype(BF16)
        bufs[3, :, here] = vacc[...].astype(BF16)
        for n, out in enumerate(outs):
            copies.append(
                pltpu.make_async_copy(bufs.at[n, :, here], out.at[:, cols(h)], sems.at[i, n])
            )
            copies[-1].start()
        for t in range(PICK):
            rows = pl.ds(pl.multiple_of(t * DILATION + group * 8, 8), 8)
            tiles[0, t, :, here] = kacc[rows, :] * SCALE
            tiles[1, t, :, here] = vacc[rows, :]
    for copy in copies:
        copy.wait()


def gather_kernel(ids, mine, *refs):
    from_z, (own, back1, back2) = refs[:7], refs[7:]
    z = ids[0] & 7
    for kv in range(2):
        a, b, c = mine[0, kv], mine[1, kv], mine[2, kv]
        for k, part in zip(SHIFTS, from_z):
            up = z + k < ZN
            low = part[kv, 0:PICK].astype(F32)
            high = part[kv, PICK : 2 * PICK].astype(F32)
            a = a + jnp.where(up, low, 0.0)
            b = b + jnp.where(up, high, low)
            c = c + jnp.where(up, 0.0, high)
        own[kv] = a
        back1[kv] = b.astype(BF16)
        back2[kv] = c.astype(BF16)


def finish_kernel(
    ids, own, back1, back2, early, late, _key, _value, key_grad, value_grad, kbuf, vbuf, sems
):
    group = lax.shift_right_logical(ids[1] * HEADS, 3)
    first = (ids[1] * HEADS) & 7
    inner = lax.broadcasted_iota(jnp.int32, (PICK, 8, D), 1)
    copies = []
    for kv, buf, out in ((0, kbuf, key_grad), (1, vbuf, value_grad)):
        for h in range(HEADS):
            far = (
                own[kv, :, cols(h)]
                + back1[kv, :, cols(h)].astype(F32)
                + back2[kv, :, cols(h)].astype(F32)
            )
            wide = jnp.where(inner == first + h, far[:, None, :], 0.0)
            near = (early if h in EARLY else late)[kv, :, :, cols(h % 2)]
            buf[:, :, cols(h)] = (near + wide).astype(BF16)
        copies.append(pltpu.make_async_copy(buf, out.at[:, group], sems.at[kv]))
        copies[-1].start()
    for copy in copies:
        copy.wait()


SMEM = pl.BlockSpec(memory_space=pltpu.SMEM)
VMEM = pl.BlockSpec(memory_space=pltpu.VMEM)


ANY = pl.BlockSpec(memory_space=pltpu.HBM)


def call(kernel, specs, args, outs, scratch=(), flops=0, nbytes=0, out_specs=None, alias=None):
    specs = list(specs) + [VMEM] * (len(args) - len(specs))
    args = [
        pltpu.with_memory_space_constraint(a, pltpu.HBM) if s is ANY else a
        for a, s in zip(args, specs)
    ]
    return pl.pallas_call(
        kernel,
        out_shape=tuple(jax.ShapeDtypeStruct(s, t) for s, t in outs),
        in_specs=specs,
        out_specs=tuple(out_specs or [VMEM] * len(outs)),
        scratch_shapes=scratch,
        input_output_aliases=alias or {},
        compiler_params=pltpu.CompilerParams(vmem_limit_bytes=LIMIT),
        cost_estimate=pl.CostEstimate(flops=flops, bytes_accessed=nbytes, transcendentals=0),
    )(*args)


def along_y(step):
    return [(y * ZN + z, (y + step) % YN * ZN + z) for y in range(YN) for z in range(ZN)]


def along_z(step):
    return [(y * ZN + z, y * ZN + (z + step) % ZN) for y in range(YN) for z in range(ZN)]


def along_x(step):
    return [(p, (p + 2 * step) % 8) for p in range(8)]


def shards(queries, keys, values, out_grad, norm_gain, doc_lengths, group_level):
    two = jnp.arange(2, dtype=jnp.int32)
    ids = jnp.where(two == 0, lax.axis_index("ctx"), lax.axis_index("head")).astype(jnp.int32)
    gain = norm_gain.reshape(1, WIDE)
    bundle = (2, PICK, WIDE)
    column = (2, 2 * PICK, WIDE)
    square = (TOK, WIDE)
    tiled = (PICK, DILATION // 8, 8, WIDE)
    tile = (PICK, 8, WIDE)

    (mine,) = call(
        pick_kernel,
        [SMEM, ANY, ANY],
        (ids, keys.reshape(tiled), values.reshape(tiled)),
        [(bundle, BF16)],
        scratch=[pltpu.VMEM(tile, BF16), pltpu.VMEM(tile, BF16), pltpu.SemaphoreType.DMA((2,))],
        nbytes=1 << 18,
    )
    r1 = lax.ppermute(mine, "ctx", along_y(1))
    r2 = lax.ppermute(mine, "ctx", along_y(2))
    scaled, fbias, nbias, grads, q, k, v, gain = call(
        prepare_kernel,
        [SMEM] + [ANY] * 7,
        (ids, doc_lengths, group_level, queries, keys, values, out_grad, gain),
        [
            ((WIDE, TOK), F32), ((HEADS, FAR, TOK), F32), ((TOK, TOK), F32), ((8, TOK), F32),
            (square, BF16), (square, BF16), (square, BF16), ((1, WIDE), F32),
        ],
        scratch=[
            pltpu.VMEM(square, BF16), pltpu.SMEM((DOCS,), jnp.int32), pltpu.SMEM((8,), jnp.int32),
            pltpu.SemaphoreType.DMA((7,)),
        ],
        flops=4 * TOK * TOK * D,
        nbytes=4 << 20,
    )
    r1, r2, nbias = lax.optimization_barrier((r1, r2, nbias))
    sent = call(
        bundle_kernel, [SMEM], (ids, mine, r1, r2), [(column, BF16)] * 7, nbytes=1 << 19
    )
    got = [lax.ppermute(a, "ctx", along_z(k)) for k, a in zip(SHIFTS, sent)]
    *_, later_ids = lax.optimization_barrier((*sent, ids))
    acc, rows = call(
        near_forward_kernel,
        [SMEM],
        (later_ids, nbias, grads, q, k, v),
        [((WIDE, TOK), F32), ((16, TOK), F32)],
        flops=4 * 4 * TOK * TOK * D,
        nbytes=4 << 20,
    )
    flat, stats, totals, fk, fv = call(
        far_forward_kernel,
        [],
        (*got, mine, r1, r2, q, acc, rows, scaled, fbias),
        [
            ((WIDE, TOK), BF16), ((8, TOK), F32), ((8, TOK), F32),
            ((FAR, WIDE), BF16), ((FAR, WIDE), BF16),
        ],
        flops=4 * 4 * TOK * FAR * D,
        nbytes=4 << 20,
    )
    s0 = stats + lax.ppermute(stats, "head", [(p, p ^ 1) for p in range(8)])
    s1, s2, s3 = (lax.ppermute(s0, "head", along_x(k)) for k in (1, 2, 3))
    _, later = lax.optimization_barrier((s0, totals))
    far_weight, near_weight = call(
        weight_kernel,
        [],
        (fk, q, k, later, fbias, nbias),
        [((HEADS, FAR, TOK), F32), ((HEADS, TOK, TOK), F32)],
        flops=2 * 4 * TOK * FAR * D,
        nbytes=4 << 20,
    )
    *back, back_own = call(
        far_backward_kernel,
        [],
        (s0, s1, s2, s3, fv, q, flat, scaled, far_weight),
        [(column, BF16)] * 7 + [((3, *bundle), F32)],
        scratch=[pltpu.VMEM((FAR, D), F32), pltpu.VMEM((FAR, D), F32)],
        flops=8 * 4 * TOK * FAR * D,
        nbytes=4 << 20,
    )
    to_send = dict(zip(SHIFTS, back))
    home = {k: lax.ppermute(to_send[k], "ctx", along_z(-k)) for k in BACK_SHIFTS}
    arrived = [home[k] for k in SHIFTS]
    *_, later_ids = lax.optimization_barrier((*back, ids))
    operands = (s0, s1, s2, s3, fk, fv, q, k, v, flat, scaled, far_weight, near_weight, gain)
    near_scratch = [
        pltpu.VMEM((TOK, D), F32), pltpu.VMEM((TOK, D), F32),
        pltpu.VMEM((4, TOK, 2 * D), BF16), pltpu.SemaphoreType.DMA((2, 4)),
    ]
    halves = [(square, BF16)] * 4 + [((2, PICK, 8, 2 * D), F32)]
    *partial, early = call(
        functools.partial(near_backward_kernel, EARLY),
        [SMEM],
        (later_ids, *operands),
        halves,
        scratch=near_scratch,
        out_specs=[ANY] * 4 + [VMEM],
        flops=8 * 4 * TOK * TOK * D,
        nbytes=4 << 20,
    )
    *arrived, early = lax.optimization_barrier((*arrived, early))
    own, back1, back2 = call(
        gather_kernel,
        [SMEM],
        (ids, back_own, *arrived),
        [(bundle, F32), (bundle, BF16), (bundle, BF16)],
        nbytes=1 << 20,
    )
    _, later_ids = lax.optimization_barrier((back1, ids))
    back1 = lax.ppermute(back1, "ctx", along_y(-1))
    back2 = lax.ppermute(back2, "ctx", along_y(-2))
    output, query_grad, key_grad, value_grad, late = call(
        functools.partial(near_backward_kernel, LATE),
        [SMEM] + [VMEM] * 14 + [ANY] * 4,
        (later_ids, *operands, *partial),
        halves,
        scratch=near_scratch,
        out_specs=[ANY] * 4 + [VMEM],
        alias={15: 0, 16: 1, 17: 2, 18: 3},
        flops=8 * 4 * TOK * TOK * D,
        nbytes=4 << 20,
    )
    key_grad, value_grad = call(
        finish_kernel,
        [SMEM, VMEM, VMEM, VMEM, VMEM, VMEM, ANY, ANY],
        (ids, own, back1, back2, early, late, key_grad.reshape(tiled), value_grad.reshape(tiled)),
        [(tiled, BF16), (tiled, BF16)],
        scratch=[pltpu.VMEM(tile, BF16), pltpu.VMEM(tile, BF16), pltpu.SemaphoreType.DMA((2,))],
        out_specs=[ANY, ANY],
        alias={6: 0, 7: 1},
        nbytes=1 << 18,
    )
    return output, query_grad, key_grad.reshape(square), value_grad.reshape(square)


def solution(mesh):
    tokens = P("ctx", "head")
    return jax.shard_map(
        shards,
        mesh=mesh,
        in_specs=(tokens, tokens, tokens, tokens, P("head"), P(), P()),
        out_specs=(tokens, tokens, tokens, tokens),
        check_vma=False,
    )
```

```python
import functools

import jax
import jax.numpy as jnp
from jax import lax
from jax.experimental import pallas as pl
from jax.experimental.pallas import tpu as pltpu
from jax.sharding import PartitionSpec as P

D = 128
HEADS = 4
TOK = 512
WIDE = HEADS * D
DILATION = 32
DOCS = 16
PICK = TOK // DILATION
ZN = 8
YN = 4
FAR = 17 * PICK
HALF = 256
SPAN = 512
FULL = 4096.0
EPS = 1e-05
SCALE = D ** (-0.5)
C2 = SCALE * 1.4426950408889634
NEG = -1e30
LIMIT = 8 << 20
SHIFTS = (4, 3, 5, 2, 6, 1, 7)
BACK_SHIFTS = (4, 3, 5, 2, 6, 1, 7)


F32 = jnp.float32
BF16 = jnp.bfloat16


def nn(a, b):
    return lax.dot_general(a, b, (((1,), (0,)), ((), ())), preferred_element_type=F32)


def nt(a, b):
    return lax.dot_general(a, b, (((1,), (1,)), ((), ())), preferred_element_type=F32)


def tn(a, b):
    return lax.dot_general(a, b, (((0,), (0,)), ((), ())), preferred_element_type=F32)


EARLY, LATE = (0, 1), (2, 3)


def cols(h):
    return slice(h * D, (h + 1) * D)


def query_rows(ids, lens):
    place = ids[0] * TOK + lax.broadcasted_iota(jnp.int32, (1, TOK), 1)
    start = jnp.zeros((1, TOK), jnp.int32)
    end = jnp.int32(0)
    for k in range(DOCS):
        end = end + lens[k]
        start = jnp.where(place >= end, end, start)
    return place, start


def near_bias(place, start, at, depth):
    base = place[:, 0:1]
    key = lax.broadcasted_iota(jnp.int32, (depth, HALF), 0)
    query = place[:, at : at + HALF] - base
    first = start[:, at : at + HALF] - base
    return jnp.where((key <= query) & (key >= first), 0.0, NEG)


def far_places(ids, levels):
    row = lax.broadcasted_iota(jnp.int32, (FAR, 1), 0)
    block = lax.shift_right_logical(row, 4)
    t = row & 15
    z = ids[0] & 7
    y = lax.shift_right_logical(ids[0], 3)
    pair = lax.shift_right_logical(block, 1)
    shift = jnp.zeros_like(pair)
    for i, k in enumerate(SHIFTS):
        shift = jnp.where(pair == i, k, shift)
    from_z = (z - shift) & 7
    at = (y - (block & 1) - jnp.where(from_z > z, 1, 0)) * ZN + from_z
    at = jnp.where(block >= 14, (y - (block - 14)) * ZN + z, at)
    rate = lax.shift_left(jnp.int32(1), levels[ids[1]])
    return jnp.where((t & (rate - 1)) == 0, at * TOK + t * DILATION, -(1 << 29))


def pick_kernel(ids, k, v, out, kbuf, vbuf, sems):
    group = lax.shift_right_logical(ids[1] * HEADS, 3)
    copies = [
        pltpu.make_async_copy(k.at[:, group], kbuf, sems.at[0]),
        pltpu.make_async_copy(v.at[:, group], vbuf, sems.at[1]),
    ]
    for copy in copies:
        copy.start()
    row = lax.broadcasted_iota(jnp.int32, (PICK, PICK * 8), 0) * 8
    col = lax.broadcasted_iota(jnp.int32, (PICK, PICK * 8), 1)
    first = (ids[1] * HEADS) & 7
    for kv, buf in enumerate((kbuf, vbuf)):
        copies[kv].wait()
        for h in range(HEADS):
            one = jnp.where(col == row + (first + h), 1.0, 0.0).astype(BF16)
            rows = buf[:, :, cols(h)].astype(F32).reshape(PICK * 8, D).astype(BF16)
            out[kv, :, cols(h)] = nn(one, rows).astype(BF16)


def bundle_kernel(ids, own, r1, r2, *outs):
    z = ids[0] & 7
    for k, out in zip(SHIFTS, outs):
        up = z + k < ZN
        out[:, 0:PICK] = jnp.where(up, own[...], r1[...])
        out[:, PICK : 2 * PICK] = jnp.where(up, r1[...], r2[...])


def prepare_kernel(
    ids, lens_at, levels_at, q_at, k_at, v_at, g_at, gain_at,
    scaled, fbias, nbias, grads, q, k, v, gain, g, lens, levels, sems,
):
    pairs = (
        (lens_at, lens), (levels_at, levels), (g_at, g), (gain_at, gain), (q_at, q), (k_at, k),
        (v_at, v),
    )
    copies = [pltpu.make_async_copy(a, b, sems.at[i]) for i, (a, b) in enumerate(pairs)]
    for copy in copies:
        copy.start()
    for copy in copies[:2]:
        copy.wait()
    place, start = query_rows(ids, lens)
    fplace = far_places(ids, levels)
    for h in range(HEADS):
        offset = ids[1] * HEADS + h
        live = (fplace <= place - offset) & (fplace >= start - offset)
        fbias[h] = jnp.where(live, 0.0, NEG)
    for at in range(0, TOK, HALF):
        nbias[: at + HALF, at : at + HALF] = near_bias(place, start, at, at + HALF)
    nbias[HALF:, :HALF] = jnp.full((HALF, HALF), NEG, F32)
    for copy in copies[2:4]:
        copy.wait()
    total = jnp.zeros((1, TOK), F32)
    for h in range(HEADS):
        part = (g[:, cols(h)].astype(F32) * gain[:, cols(h)]).T
        scaled[cols(h), :] = part
        total = total + jnp.sum(part, axis=0, keepdims=True)
    grads[0:1, :] = total
    grads[1:8, :] = jnp.zeros((7, TOK), F32)
    for copy in copies[4:]:
        copy.wait()


def near_forward_kernel(ids, nbias, grads, q, k, v, acc, rows):
    for h in range(HEADS):
        for at in range(0, TOK, HALF):
            depth = at + HALF
            s = nt(k[:depth, cols(h)], q[at:depth, cols(h)]) * C2 + nbias[:depth, at:depth]
            top = jnp.max(s, axis=0, keepdims=True)
            p = jnp.exp2(s - top)
            rows[h : h + 1, at:depth] = top
            rows[HEADS + h : HEADS + h + 1, at:depth] = jnp.sum(p, axis=0, keepdims=True)
            acc[cols(h), at:depth] = tn(v[:depth, cols(h)], p.astype(BF16))
    rows[8:16, :] = grads[...]


def far_forward_kernel(*refs):
    from_z, refs = refs[:7], refs[7:]
    own, r1, r2, q, acc, rows, scaled, fbias, flat, stats, totals, fk, fv = refs
    for kv, out in ((0, fk), (1, fv)):
        for i, a in enumerate(from_z):
            out[i * 2 * PICK : (i + 1) * 2 * PICK, :] = a[kv]
        for i, a in enumerate((own, r1, r2)):
            out[14 * PICK + i * PICK : 15 * PICK + i * PICK, :] = a[kv]
    for at in range(0, TOK, SPAN):
        part = slice(at, at + SPAN)
        sums = jnp.zeros((1, SPAN), F32)
        squares = jnp.zeros((1, SPAN), F32)
        cross = jnp.zeros((1, SPAN), F32)
        for h in range(HEADS):
            s = nt(fk[:, cols(h)], q[part, cols(h)]) * C2 + fbias[h, :, part]
            near_top = rows[h : h + 1, part]
            top = jnp.maximum(near_top, jnp.max(s, axis=0, keepdims=True))
            p = jnp.exp2(s - top)
            shrink = jnp.exp2(near_top - top)
            total = rows[HEADS + h : HEADS + h + 1, part] * shrink + jnp.sum(
                p, axis=0, keepdims=True
            )
            o = acc[cols(h), part] * shrink + tn(fv[:, cols(h)], p.astype(BF16))
            o = (o * (1.0 / total)).astype(BF16)
            flat[cols(h), part] = o
            totals[h : h + 1, part] = top + jnp.log2(total)
            f = o.astype(F32)
            sums = sums + jnp.sum(f, axis=0, keepdims=True)
            squares = squares + jnp.sum(f * f, axis=0, keepdims=True)
            cross = cross + jnp.sum(f * scaled[cols(h), part], axis=0, keepdims=True)
        stats[0:1, part] = sums
        stats[1:2, part] = squares
        stats[2:3, part] = rows[8:9, part]
        stats[3:4, part] = cross
    stats[4:8, :] = jnp.zeros((4, TOK), F32)
    totals[4:8, :] = jnp.zeros((4, TOK), F32)


def weight_kernel(far_keys, q, k, totals, fbias, nbias, far_weight, near_weight):
    for h in range(HEADS):
        fk = far_keys[:, cols(h)]
        for at in range(0, TOK, HALF):
            depth = at + HALF
            total = totals[h : h + 1, at:depth]
            qh = q[at:depth, cols(h)]
            far_weight[h, :, at:depth] = jnp.exp2(nt(fk, qh) * C2 + fbias[h, :, at:depth] - total)
            near_weight[h, :depth, at:depth] = jnp.exp2(
                nt(k[:depth, cols(h)], qh) * C2 + nbias[:depth, at:depth] - total
            )


def norm_rows(s0, s1, s2, s3, part):
    tot = (s0[:, part] + s1[:, part]) + (s2[:, part] + s3[:, part])
    mean = tot[0:1] / FULL
    rstd = lax.rsqrt(tot[1:2] / FULL - mean * mean + EPS)
    grad_mean = tot[2:3] / FULL
    grad_proj = rstd * (tot[3:4] - mean * tot[2:3]) / FULL
    return mean, rstd, grad_mean, grad_proj


def att_grad_of(flat, scaled, norm, h, part):
    mean, rstd, grad_mean, grad_proj = norm
    f = flat[cols(h), part].astype(F32)
    normed = (f - mean) * rstd
    grad = (rstd * (scaled[cols(h), part] - grad_mean - normed * grad_proj)).astype(BF16)
    delta = jnp.sum(grad.astype(F32) * f, axis=0, keepdims=True)
    return grad, delta, normed


def far_backward_kernel(s0, s1, s2, s3, fv, q, flat, scaled, weight, *refs):
    outs, (own, kacc, vacc) = refs[:7], refs[7:]
    for h in range(HEADS):
        key_part = jnp.zeros((FAR, D), F32)
        value_part = jnp.zeros((FAR, D), F32)
        for at in range(0, TOK, HALF):
            part = slice(at, at + HALF)
            norm = norm_rows(s0, s1, s2, s3, part)
            grad, delta, _ = att_grad_of(flat, scaled, norm, h, part)
            p = weight[h, :, part]
            slope = (p * (nn(fv[:, cols(h)], grad) - delta)).astype(BF16)
            key_part = key_part + nn(slope, q[part, cols(h)])
            value_part = value_part + nt(p.astype(BF16), grad)
        kacc[...] = key_part * SCALE
        vacc[...] = value_part
        for kv, grads in ((0, kacc), (1, vacc)):
            for i, out in enumerate(outs):
                out[kv, :, cols(h)] = grads[i * 2 * PICK : (i + 1) * 2 * PICK, :].astype(BF16)
            for i in range(3):
                own[i, kv, :, cols(h)] = grads[(14 + i) * PICK : (15 + i) * PICK, :]


def near_backward_kernel(heads, ids, *refs):
    s0, s1, s2, s3, fk, fv, q, k, v, flat, scaled, far_weight, near_weight, gain = refs[:14]
    outs, (tiles, kacc, vacc, bufs, sems) = refs[-9:-5], refs[-5:]
    group = lax.shift_right_logical(ids[1] * HEADS, 3)
    norms = [norm_rows(s0, s1, s2, s3, slice(at, at + HALF)) for at in range(0, TOK, HALF)]
    copies = []
    for i, h in enumerate(heads):
        here = cols(i)
        for at in range(0, TOK, HALF):
            part = slice(at, at + HALF)
            depth = at + HALF
            grad, delta, normed = att_grad_of(flat, scaled, norms[at // HALF], h, part)
            bufs[0, part, here] = (normed.T * gain[:, cols(h)]).astype(BF16)
            qh = q[part, cols(h)]
            kh, vh = k[:depth, cols(h)], v[:depth, cols(h)]
            p = near_weight[h, :depth, part]
            slope = (p * (nn(vh, grad) - delta)).astype(BF16)
            key_part = nn(slope, qh)
            value_part = nt(p.astype(BF16), grad)
            if at == 0:
                kacc[:depth, :] = key_part
                vacc[:depth, :] = value_part
            else:
                kacc[:at, :] += key_part[:at]
                vacc[:at, :] += value_part[:at]
                kacc[at:, :] = key_part[at:]
                vacc[at:, :] = value_part[at:]
            query_part = tn(kh, slope)
            slope = (far_weight[h, :, part] * (nn(fv[:, cols(h)], grad) - delta)).astype(BF16)
            query_part = query_part + tn(fk[:, cols(h)], slope)
            bufs[1, part, here] = (query_part.T * SCALE).astype(BF16)
        bufs[2, :, here] = (kacc[...] * SCALE).astype(BF16)
        bufs[3, :, here] = vacc[...].astype(BF16)
        for n, out in enumerate(outs):
            copies.append(
                pltpu.make_async_copy(bufs.at[n, :, here], out.at[:, cols(h)], sems.at[i, n])
            )
            copies[-1].start()
        for t in range(PICK):
            rows = pl.ds(pl.multiple_of(t * DILATION + group * 8, 8), 8)
            tiles[0, t, :, here] = kacc[rows, :] * SCALE
            tiles[1, t, :, here] = vacc[rows, :]
    for copy in copies:
        copy.wait()


def gather_kernel(ids, mine, *refs):
    from_z, (own, back1, back2) = refs[:7], refs[7:]
    z = ids[0] & 7
    for kv in range(2):
        a, b, c = mine[0, kv], mine[1, kv], mine[2, kv]
        for k, part in zip(SHIFTS, from_z):
            up = z + k < ZN
            low = part[kv, 0:PICK].astype(F32)
            high = part[kv, PICK : 2 * PICK].astype(F32)
            a = a + jnp.where(up, low, 0.0)
            b = b + jnp.where(up, high, low)
            c = c + jnp.where(up, 0.0, high)
        own[kv] = a
        back1[kv] = b.astype(BF16)
        back2[kv] = c.astype(BF16)


def finish_kernel(
    ids, own, back1, back2, early, late, _key, _value, key_grad, value_grad, kbuf, vbuf, sems
):
    group = lax.shift_right_logical(ids[1] * HEADS, 3)
    first = (ids[1] * HEADS) & 7
    inner = lax.broadcasted_iota(jnp.int32, (PICK, 8, D), 1)
    copies = []
    for kv, buf, out in ((0, kbuf, key_grad), (1, vbuf, value_grad)):
        for h in range(HEADS):
            far = (
                own[kv, :, cols(h)]
                + back1[kv, :, cols(h)].astype(F32)
                + back2[kv, :, cols(h)].astype(F32)
            )
            wide = jnp.where(inner == first + h, far[:, None, :], 0.0)
            near = (early if h in EARLY else late)[kv, :, :, cols(h % 2)]
            buf[:, :, cols(h)] = (near + wide).astype(BF16)
        copies.append(pltpu.make_async_copy(buf, out.at[:, group], sems.at[kv]))
        copies[-1].start()
    for copy in copies:
        copy.wait()


SMEM = pl.BlockSpec(memory_space=pltpu.SMEM)
VMEM = pl.BlockSpec(memory_space=pltpu.VMEM)


ANY = pl.BlockSpec(memory_space=pltpu.HBM)


def call(kernel, specs, args, outs, scratch=(), flops=0, nbytes=0, out_specs=None, alias=None):
    specs = list(specs) + [VMEM] * (len(args) - len(specs))
    args = [
        pltpu.with_memory_space_constraint(a, pltpu.HBM) if s is ANY else a
        for a, s in zip(args, specs)
    ]
    return pl.pallas_call(
        kernel,
        out_shape=tuple(jax.ShapeDtypeStruct(s, t) for s, t in outs),
        in_specs=specs,
        out_specs=tuple(out_specs or [VMEM] * len(outs)),
        scratch_shapes=scratch,
        input_output_aliases=alias or {},
        compiler_params=pltpu.CompilerParams(vmem_limit_bytes=LIMIT),
        cost_estimate=pl.CostEstimate(flops=flops, bytes_accessed=nbytes, transcendentals=0),
    )(*args)


def along_y(step):
    return [(y * ZN + z, (y + step) % YN * ZN + z) for y in range(YN) for z in range(ZN)]


def along_z(step):
    return [(y * ZN + z, y * ZN + (z + step) % ZN) for y in range(YN) for z in range(ZN)]


def along_x(step):
    return [(p, (p + 2 * step) % 8) for p in range(8)]


def shards(queries, keys, values, out_grad, norm_gain, doc_lengths, group_level):
    two = jnp.arange(2, dtype=jnp.int32)
    ids = jnp.where(two == 0, lax.axis_index("ctx"), lax.axis_index("head")).astype(jnp.int32)
    gain = norm_gain.reshape(1, WIDE)
    bundle = (2, PICK, WIDE)
    column = (2, 2 * PICK, WIDE)
    square = (TOK, WIDE)
    tiled = (PICK, DILATION // 8, 8, WIDE)
    tile = (PICK, 8, WIDE)

    (mine,) = call(
        pick_kernel,
        [SMEM, ANY, ANY],
        (ids, keys.reshape(tiled), values.reshape(tiled)),
        [(bundle, BF16)],
        scratch=[pltpu.VMEM(tile, BF16), pltpu.VMEM(tile, BF16), pltpu.SemaphoreType.DMA((2,))],
        nbytes=1 << 18,
    )
    r1 = lax.ppermute(mine, "ctx", along_y(1))
    r2 = lax.ppermute(mine, "ctx", along_y(2))
    scaled, fbias, nbias, grads, q, k, v, gain = call(
        prepare_kernel,
        [SMEM] + [ANY] * 7,
        (ids, doc_lengths, group_level, queries, keys, values, out_grad, gain),
        [
            ((WIDE, TOK), F32), ((HEADS, FAR, TOK), F32), ((TOK, TOK), F32), ((8, TOK), F32),
            (square, BF16), (square, BF16), (square, BF16), ((1, WIDE), F32),
        ],
        scratch=[
            pltpu.VMEM(square, BF16), pltpu.SMEM((DOCS,), jnp.int32), pltpu.SMEM((8,), jnp.int32),
            pltpu.SemaphoreType.DMA((7,)),
        ],
        flops=4 * TOK * TOK * D,
        nbytes=4 << 20,
    )
    r1, r2, nbias = lax.optimization_barrier((r1, r2, nbias))
    sent = call(
        bundle_kernel, [SMEM], (ids, mine, r1, r2), [(column, BF16)] * 7, nbytes=1 << 19
    )
    got = [lax.ppermute(a, "ctx", along_z(k)) for k, a in zip(SHIFTS, sent)]
    *_, later_ids = lax.optimization_barrier((*sent, ids))
    acc, rows = call(
        near_forward_kernel,
        [SMEM],
        (later_ids, nbias, grads, q, k, v),
        [((WIDE, TOK), F32), ((16, TOK), F32)],
        flops=4 * 4 * TOK * TOK * D,
        nbytes=4 << 20,
    )
    flat, stats, totals, fk, fv = call(
        far_forward_kernel,
        [],
        (*got, mine, r1, r2, q, acc, rows, scaled, fbias),
        [
            ((WIDE, TOK), BF16), ((8, TOK), F32), ((8, TOK), F32),
            ((FAR, WIDE), BF16), ((FAR, WIDE), BF16),
        ],
        flops=4 * 4 * TOK * FAR * D,
        nbytes=4 << 20,
    )
    s0 = stats + lax.ppermute(stats, "head", [(p, p ^ 1) for p in range(8)])
    s2, s1, s3 = (lax.ppermute(s0, "head", along_x(k)) for k in (2, 1, 3))
    _, later = lax.optimization_barrier((s0, totals))
    far_weight, near_weight = call(
        weight_kernel,
        [],
        (fk, q, k, later, fbias, nbias),
        [((HEADS, FAR, TOK), F32), ((HEADS, TOK, TOK), F32)],
        flops=2 * 4 * TOK * FAR * D,
        nbytes=4 << 20,
    )
    *back, back_own = call(
        far_backward_kernel,
        [],
        (s0, s1, s2, s3, fv, q, flat, scaled, far_weight),
        [(column, BF16)] * 7 + [((3, *bundle), F32)],
        scratch=[pltpu.VMEM((FAR, D), F32), pltpu.VMEM((FAR, D), F32)],
        flops=8 * 4 * TOK * FAR * D,
        nbytes=4 << 20,
    )
    to_send = dict(zip(SHIFTS, back))
    home = {k: lax.ppermute(to_send[k], "ctx", along_z(-k)) for k in BACK_SHIFTS}
    arrived = [home[k] for k in SHIFTS]
    *_, later_ids = lax.optimization_barrier((*back, ids))
    operands = (s0, s1, s2, s3, fk, fv, q, k, v, flat, scaled, far_weight, near_weight, gain)
    near_scratch = [
        pltpu.VMEM((TOK, D), F32), pltpu.VMEM((TOK, D), F32),
        pltpu.VMEM((4, TOK, 2 * D), BF16), pltpu.SemaphoreType.DMA((2, 4)),
    ]
    halves = [(square, BF16)] * 4 + [((2, PICK, 8, 2 * D), F32)]
    *partial, early = call(
        functools.partial(near_backward_kernel, EARLY),
        [SMEM],
        (later_ids, *operands),
        halves,
        scratch=near_scratch,
        out_specs=[ANY] * 4 + [VMEM],
        flops=8 * 4 * TOK * TOK * D,
        nbytes=4 << 20,
    )
    *arrived, early = lax.optimization_barrier((*arrived, early))
    own, back1, back2 = call(
        gather_kernel,
        [SMEM],
        (ids, back_own, *arrived),
        [(bundle, F32), (bundle, BF16), (bundle, BF16)],
        nbytes=1 << 20,
    )
    _, later_ids = lax.optimization_barrier((back1, ids))
    back2 = lax.ppermute(back2, "ctx", along_y(-2))
    back1 = lax.ppermute(back1, "ctx", along_y(-1))
    output, query_grad, key_grad, value_grad, late = call(
        functools.partial(near_backward_kernel, LATE),
        [SMEM] + [VMEM] * 14 + [ANY] * 4,
        (later_ids, *operands, *partial),
        halves,
        scratch=near_scratch,
        out_specs=[ANY] * 4 + [VMEM],
        alias={15: 0, 16: 1, 17: 2, 18: 3},
        flops=8 * 4 * TOK * TOK * D,
        nbytes=4 << 20,
    )
    key_grad, value_grad = call(
        finish_kernel,
        [SMEM, VMEM, VMEM, VMEM, VMEM, VMEM, ANY, ANY],
        (ids, own, back1, back2, early, late, key_grad.reshape(tiled), value_grad.reshape(tiled)),
        [(tiled, BF16), (tiled, BF16)],
        scratch=[pltpu.VMEM(tile, BF16), pltpu.VMEM(tile, BF16), pltpu.SemaphoreType.DMA((2,))],
        out_specs=[ANY, ANY],
        alias={6: 0, 7: 1},
        nbytes=1 << 18,
    )
    return output, query_grad, key_grad.reshape(square), value_grad.reshape(square)


def solution(mesh):
    tokens = P("ctx", "head")
    return jax.shard_map(
        shards,
        mesh=mesh,
        in_specs=(tokens, tokens, tokens, tokens, P("head"), P(), P()),
        out_specs=(tokens, tokens, tokens, tokens),
        check_vma=False,
    )
```
